32 devices in a mesh: scen: 2 (over y), orig: 4 (over x, core), dest: 4 (over z).
Axes of the slice: x: 2, y: 2, z: 4, core: 2. Of those that a mesh axis runs over, the one named last changes fastest.
Arguments:
- skims: bfloat16 [12, 512, 4096], P(None, ('scen', 'orig'), 'dest'), parts along dimension 1, may hold values from -500 to 500
- coef: bfloat16 [64, 12], replicated, may hold values from -1.75 to 1.75
- asc: float32 [64], replicated, may hold values from -4 to 4
- theta: float32 [4], replicated, may hold values from 0.5 to 1
- beta: float32 [4, 10], replicated, may hold values from 0.01 to 1
- employment: int32 [10, 8192], P(None, ('scen', 'dest')), parts along dimension 1, may hold values from 1 to 2000
- zone_district: int32 [4096], P('dest'), may hold values from 0 to 63
- anchor_district: int32 [512], P(('scen', 'orig')), parts along dimension 0, may hold values from 0 to 63
- district_const: float32 [64, 64], replicated, may hold values from -3 to 3
- segment: int32 [512], P(('scen', 'orig')), parts along dimension 0, may hold values from 0 to 3
- availability: int32 [512, 16], P(('scen', 'orig')), parts along dimension 0, may hold values 0 or 1
- workers: float32 [512], P(('scen', 'orig')), parts along dimension 0, may hold values from 50 to 1500
Outputs:
- accessibility: float32 [512], P(('scen', 'orig')), parts along dimension 0
- flow_table: float32 [512, 1024], P(('scen', 'orig')), parts along dimension 0
- modelled: float32 [4, 8192], P(None, ('scen', 'dest')), parts along dimension 1
- shadow: float32 [4, 8192], P(None, ('scen', 'dest')), parts along dimension 1
The draws below stay inside these ranges and needn't reach their ends.
There are 2 independent parts, one for each index of `scen`. The reference program is written for one: setup_inputs(seed, part) draws one part's arguments, and reference() takes and returns one part's arrays. A program takes and returns all parts, laid end to end along the dimension named above; an argument that names none is the same for every part. Nothing has to cross between parts.
All inputs are finite; a program needn't handle non-finite values. No bound on the sum of `availability` on one device may be relied on, other than what follows from the above.
Results may differ from the reference program's by a relative error of at most 0.0003.
Values sent between devices are 32-bit elements; how exact they have to be, the bound alone decides.
A program may use at most 64 MiB of HBM per device.

```python
import math
import jax
import jax.numpy as jnp
from jax import lax

K = 12
S = 4
M = 16
C = 10
ND = 64
ITERS = 2
ORIG_DEV = 64
ZONES = 4096
ANCHORS = 256
P_SIZE = 64
N_ORIG = 4


def draw_skims(key, part):
    first_key = jax.random.fold_in(jax.random.fold_in(key, 11), 0)
    values = jnp.clip(jax.random.normal(first_key, (K, ANCHORS, ZONES), jnp.float32), -5.0, 5.0)
    return values.astype(jnp.bfloat16)


def touch_ends(entries, stream_key, smallest, high):
    longest = entries.shape.index(max(entries.shape))
    spots = []
    for shift in (0, 1):
        where = [jax.random.randint(jax.random.fold_in(stream_key, axis), (), 0, length) for axis, length in enumerate(entries.shape)]
        where[longest] = (where[longest] + shift) % entries.shape[longest]
        spots.append(tuple(where))
    return entries.at[spots[0]].set(smallest).at[spots[1]].set(high)


def shard_levels(stream_key, dims, pieces, low, largest):
    level, own = 1.0, jax.random.fold_in(stream_key, 6)
    for dim, parts in pieces:
        heights = jnp.exp(jax.random.uniform(jax.random.fold_in(own, dim), (parts,), jnp.float32, low / len(pieces), largest / len(pieces)))
        level = level * jnp.repeat(heights, dims[dim] // parts).reshape([-1 if axis == dim else 1 for axis in range(len(dims))])
    return level


def noise(own_key, dims, width, bound, kind=jnp.bfloat16):
    values = jax.random.normal(own_key, dims, jnp.float32) * width
    return jnp.minimum(jnp.maximum(values, -bound), bound).astype(kind)


def setup_inputs(seed: int = 0, part: int = 0) -> dict:
    key_list = jax.random.split(jax.random.key(seed), 13)
    part_splits = jax.random.split(jax.random.fold_in(key_list[12], part), 13)
    skims = draw_skims(jax.random.fold_in(jax.random.fold_in(key_list[12], part), 71), part)
    coef = noise(key_list[1], (P_SIZE, K), K ** -0.5, 1.75)
    asc = noise(key_list[2], (P_SIZE,), 1.0, 4.0, jnp.float32)
    theta = jnp.clip(jax.random.uniform(key_list[3], (S,), jnp.float32, 0.5, 1.0), 0.5, 1.0)
    beta = jnp.clip(jnp.exp(jax.random.uniform(key_list[4], (S, C), jnp.float32, math.log(0.01), math.log(1.0))), 0.01, 1.0)
    employment = touch_ends(jax.random.randint(part_splits[5], (C, ZONES), 1, 2001), jax.random.fold_in(part_splits[5], 1), 1, 2000).astype(jnp.int32)
    zone_district = touch_ends(jax.random.randint(key_list[6], (ZONES,), 0, ND), jax.random.fold_in(key_list[6], 1), 0, ND - 1).astype(jnp.int32)
    anchor_district = touch_ends(jax.random.randint(part_splits[7], (ANCHORS,), 0, ND), jax.random.fold_in(part_splits[7], 1), 0, ND - 1).astype(jnp.int32)
    district_const = noise(key_list[8], (ND, ND), 0.5, 3.0, jnp.float32)
    segment = touch_ends(jax.random.randint(part_splits[9], (ANCHORS,), 0, S), jax.random.fold_in(part_splits[9], 1), 0, S - 1).astype(jnp.int32)
    availability = touch_ends((jax.random.randint(part_splits[10], (ANCHORS, M), 0, 3) < 2).astype(jnp.int32), jax.random.fold_in(part_splits[10], 1), 0, 1)
    workers = jnp.clip(jnp.exp(math.log(1500.0) - 3.4011974 * jax.random.uniform(part_splits[11], (ANCHORS,), jnp.float32) ** shard_levels(part_splits[11], (ANCHORS,), ((0, 4),), -0.2, 0.2)), 50.0, 1500.0)
    return {"skims": skims, "coef": coef, "asc": asc, "theta": theta, "beta": beta, "employment": employment, "zone_district": zone_district, "anchor_district": anchor_district, "district_const": district_const, "segment": segment, "availability": availability, "workers": workers}


HIGH = lax.Precision.HIGHEST


def reference(skims, coef, asc, theta, beta, employment, zone_district, anchor_district, district_const, segment, availability, workers):
    skim_count = skims.shape[0]
    anchor_count = skims.shape[1]
    zone_count = skims.shape[2]
    seg_count = theta.shape[0]
    mode_count = coef.shape[0] // seg_count
    dist_count = district_const.shape[0]
    coef_table = coef.reshape(seg_count, mode_count, skim_count).astype(jnp.float32)
    asc_table = asc.reshape(seg_count, mode_count)
    mode_ids = jnp.arange(mode_count, dtype=jnp.int32)
    usable = (availability > 0) | (mode_ids[None, :] == 0)

    def modes_of(start):
        skim_block = lax.dynamic_slice_in_dim(skims, start, ORIG_DEV, 1).astype(jnp.float32)
        seg_block = lax.dynamic_slice_in_dim(segment, start, ORIG_DEV, 0)
        usable_block = lax.dynamic_slice_in_dim(usable, start, ORIG_DEV, 0)
        utility = jnp.einsum("omk,kod->omd", coef_table[seg_block], skim_block, precision=HIGH)
        utility = utility + asc_table[seg_block][:, :, None]
        masked_util = jnp.where(usable_block[:, :, None], utility, -1e30)
        mode_peak = jnp.max(masked_util, axis=1)
        mode_exp = jnp.exp(masked_util - mode_peak[:, None, :])
        mode_total = jnp.sum(mode_exp, axis=1)
        return mode_peak + jnp.log(mode_total), mode_exp / mode_total[:, None, :]

    starts = jnp.arange(N_ORIG, dtype=jnp.int32) * ORIG_DEV
    logsum = lax.map(lambda start: modes_of(start)[0], starts).reshape(anchor_count, zone_count)
    size_term = jnp.dot(beta, employment.astype(jnp.float32), precision=HIGH)
    base_util = theta[segment][:, None] * logsum + jnp.log(size_term)[segment]
    base_util = base_util + district_const[anchor_district][:, zone_district]
    seg_hot = (segment[:, None] == jnp.arange(seg_count, dtype=jnp.int32)[None, :]).astype(jnp.float32)
    seg_workers = jnp.dot(workers, seg_hot, precision=HIGH)
    target = size_term * (seg_workers / jnp.sum(size_term, axis=1))[:, None]
    worker_hot = seg_hot * workers[:, None]
    shadow = jnp.zeros((seg_count, zone_count), jnp.float32)
    for iteration in range(ITERS):
        value = base_util + shadow[segment]
        peak_value = jnp.max(value, axis=1)
        dest_exp = jnp.exp(value - peak_value[:, None])
        exp_total = jnp.sum(dest_exp, axis=1)
        dest_prob = dest_exp / exp_total[:, None]
        modelled = jnp.dot(worker_hot.T, dest_prob, precision=HIGH)
        shadow = shadow + jnp.log((target + 1.0) / (modelled + 1.0))
    accessibility = peak_value + jnp.log(exp_total)
    dist_hot = (zone_district[:, None] == jnp.arange(dist_count, dtype=jnp.int32)[None, :]).astype(jnp.float32)

    def flows_of(start):
        mode_prob = modes_of(start)[1]
        prob_block = lax.dynamic_slice_in_dim(dest_prob, start, ORIG_DEV, 0)
        worker_block = lax.dynamic_slice_in_dim(workers, start, ORIG_DEV, 0)
        mixed = (prob_block * worker_block[:, None])[:, None, :] * mode_prob
        summed = jnp.einsum("omd,dg->ogm", mixed, dist_hot, precision=HIGH)
        return summed.reshape(ORIG_DEV, dist_count * mode_count)

    flow_table = lax.map(flows_of, starts).reshape(anchor_count, dist_count * mode_count)
    return accessibility, flow_table, modelled, shadow
```

```python
import functools

import jax
import jax.numpy as jnp
from jax import lax
from jax.experimental import pallas as pl
from jax.experimental.pallas import tpu as pltpu
from jax.sharding import PartitionSpec as P

HIGH = lax.Precision.HIGHEST
F32 = jnp.float32
BF16 = jnp.bfloat16
MESH = pl.DeviceIdType.MESH
GROUP = 16
TILE = 256
PIECES = 2


def iota(shape, dim):
    return lax.broadcasted_iota(jnp.int32, shape, dim)


def hot(mask, dtype=F32):
    return jnp.where(mask, 1.0, 0.0).astype(dtype)


def dot(a, b, precision=None):
    return jnp.dot(a, b, preferred_element_type=F32, precision=precision)


def dot_nt(a, b):
    return lax.dot_general(a, b, (((1,), (1,)), ((), ())), preferred_element_type=F32)


def halves(x):
    top = x.astype(BF16)
    return top, (x - top.astype(F32)).astype(BF16)


class Exchange:
    def __init__(self, axis, count, send_sem, recv_sem):
        self.axis, self.count = axis, count
        self.send_sem, self.recv_sem = send_sem, recv_sem
        self.copies = []

    def start(self, source, target, steps=None):
        me = lax.axis_index(self.axis)
        for k in range(1, self.count) if steps is None else steps:
            peer = lax.rem(me + k, self.count)
            copy = pltpu.make_async_remote_copy(
                src_ref=source(peer),
                dst_ref=target(me),
                send_sem=self.send_sem.at[k - 1],
                recv_sem=self.recv_sem.at[k - 1],
                device_id={self.axis: peer},
                device_id_type=MESH,
            )
            copy.start()
            self.copies.append(copy)

    def share(self, buf):
        me = lax.axis_index(self.axis)
        self.start(lambda peer: buf.at[me], lambda mine: buf.at[mine])

    def landed(self):
        for copy in self.copies:
            copy.wait_recv()

    def sent(self):
        for copy in self.copies:
            copy.wait_send()


def kernel(
    n_dest,
    n_orig,
    skims_hbm,
    coef_hbm,
    asc_hbm,
    theta_hbm,
    beta_hbm,
    employment_hbm,
    zone_district_hbm,
    anchor_district_hbm,
    district_const_hbm,
    segment_hbm,
    availability_hbm,
    workers_hbm,
    access_out,
    flow_out,
    modelled_out,
    shadow_out,
    skims,
    coef,
    asc,
    theta,
    beta,
    employment,
    zone_district,
    anchor_district,
    district_const,
    segment,
    availability,
    workers,
    mode_exp,
    inv_total,
    weights,
    added,
    theta_rows,
    base,
    dist_hot,
    sizes,
    segs,
    stats,
    parts,
    flows,
    flow_in,
    dest_send,
    dest_recv,
    orig_send,
    orig_recv,
    skim_sem,
    load_sem,
):
    skim_count, rows, zones = skims.shape
    seg_count = theta.shape[1]
    mode_count = availability.shape[0]
    dist_count = district_const.shape[0]
    groups = rows // GROUP
    me_dest = lax.axis_index("dest")
    me_orig = lax.axis_index("orig")
    dest = [Exchange("dest", n_dest, dest_send.at[i], dest_recv.at[i]) for i in range(3 + 2 * PIECES)]
    orig = [Exchange("orig", n_orig, orig_send.at[i], orig_recv.at[i]) for i in range(3)]

    barrier = pltpu.get_barrier_semaphore()
    for axis, me, count in (("dest", me_dest, n_dest), ("orig", me_orig, n_orig)):
        for k in range(1, count):
            pl.semaphore_signal(
                barrier,
                inc=1,
                device_id={axis: lax.rem(me + k, count)},
                device_id_type=MESH,
            )

    small = [
        (segment_hbm, segment),
        (workers_hbm, workers),
        (beta_hbm, beta),
        (employment_hbm, employment),
        (zone_district_hbm, zone_district),
        (coef_hbm, coef),
        (asc_hbm, asc),
        (availability_hbm, availability),
        (theta_hbm, theta),
        (anchor_district_hbm, anchor_district),
        (district_const_hbm, district_const),
    ]
    loads = [pltpu.make_async_copy(a, b, load_sem.at[i]) for i, (a, b) in enumerate(small)]

    def skim_load(g):
        part = pl.ds(pl.multiple_of(g * GROUP, GROUP), GROUP)
        return pltpu.make_async_copy(skims_hbm.at[:, part], skims.at[:, part], skim_sem.at[g])

    for load in loads:
        load.start()
    for g in range(groups):
        skim_load(g).start()
    for load in loads:
        load.wait()

    seg_hot_t = hot(segment[...] == iota((seg_count, rows), 0))
    worker_hot = seg_hot_t * workers[...]
    eye = hot(iota((rows, rows), 0) == iota((rows, rows), 1))
    seg_hot = dot_nt(eye.astype(BF16), seg_hot_t.astype(BF16))
    size_term = jnp.zeros((seg_count, zones), F32)
    for c in range(beta.shape[1]):
        size_term = size_term + beta[:, c : c + 1] * employment[c : c + 1, :].astype(F32)
    sizes[me_dest] = jnp.broadcast_to(jnp.sum(size_term, axis=1, keepdims=True), sizes.shape[1:])
    segs[me_orig] = jnp.broadcast_to(jnp.sum(worker_hot, axis=1, keepdims=True), segs.shape[1:])
    dist_hot[...] = hot(zone_district[...] == iota((dist_count, zones), 0), BF16)

    def by_segment(table):
        out = jnp.zeros((rows, table.shape[1]), F32)
        for s in range(seg_count):
            out = jnp.where(seg_hot[:, s : s + 1] > 0.5, table[s : s + 1, :], out)
        return out

    theta_rows[...] = jnp.broadcast_to(
        jnp.sum(seg_hot * theta[...], axis=1, keepdims=True), theta_rows.shape
    )
    anchor_hot_t = hot(anchor_district[...] == iota((dist_count, rows), 0), BF16)
    anchor_hot = dot_nt(eye.astype(BF16), anchor_hot_t)
    anchor_const = dot(anchor_hot, district_const[...], HIGH)
    top, low = halves(anchor_const)
    rest = (anchor_const - top.astype(F32) - low.astype(F32)).astype(BF16)
    pair_const = dot(jnp.concatenate([top, low, rest], axis=0), dist_hot[...])
    pair_const = pair_const[:rows] + (pair_const[rows : 2 * rows] + pair_const[2 * rows :])
    base[...] = by_segment(jnp.log(size_term)) + pair_const

    block = mode_count * GROUP
    width = skim_count * GROUP
    row = iota((groups * block, 1), 0)
    row_mode, row_anchor = row % block // GROUP, row % GROUP
    pair = seg_count * mode_count
    spread = hot(iota((seg_count, pair), 1) // mode_count == iota((seg_count, pair), 0), BF16)
    widen = hot(iota((skim_count, width), 1) // GROUP == iota((skim_count, width), 0), BF16)
    pick = hot(iota((groups * block, rows), 1) == row // block * GROUP + row_anchor, BF16)
    row_seg = dot_nt(pick, seg_hot_t.astype(BF16)).astype(BF16)
    mode_match = iota((groups * block, pair), 1) % mode_count == row_mode
    row_pair = jnp.where(mode_match, dot(row_seg, spread), 0.0)
    row_asc = jnp.sum(row_pair * asc[...], axis=1, keepdims=True)
    row_coef = dot_nt(row_pair.astype(BF16), coef[...]).astype(BF16)
    anchor_match = iota((groups * block, width), 1) % GROUP == row_anchor
    weights[...] = jnp.where(anchor_match, dot(row_coef, widen), 0.0).astype(BF16)
    open_modes = dot_nt(pick, hot(availability[...] > 0, BF16))
    own_mode = iota((groups * block, mode_count), 1) == row_mode
    usable = jnp.sum(jnp.where(own_mode, open_modes, 0.0), axis=1, keepdims=True)
    usable = usable + hot(row_mode == 0)
    added[...] = jnp.broadcast_to(
        row_asc + jnp.where(usable > 0.5, 0.0, -1e30), added.shape
    )

    def group_step(g, carry):
        first = pl.multiple_of(g * GROUP, GROUP)
        skim_load(g).wait()
        mine = pl.ds(pl.multiple_of(g * block, block), block)
        theta_col = theta_rows[pl.ds(first, GROUP), 0:1]
        for t in range(zones // TILE):
            cols = slice(t * TILE, (t + 1) * TILE)
            near = skims[:, pl.ds(first, GROUP), cols].reshape(width, TILE)
            utility = (dot(weights[mine, :], near) + added[mine, 0:1]).reshape(mode_count, GROUP, TILE)
            peak = jnp.max(utility, axis=0)
            grown = jnp.exp(utility - peak[None])
            total = jnp.sum(grown, axis=0)
            mode_exp[g, :, :, cols] = grown
            inv_total[pl.ds(first, GROUP), cols] = 1.0 / total
            base[pl.ds(first, GROUP), cols] += theta_col * (peak + jnp.log(total))
        return carry

    lax.fori_loop(0, groups, group_step, 0, unroll=True)

    pl.semaphore_wait(barrier, n_dest + n_orig - 2)
    dest[0].share(sizes)
    orig[0].share(segs)

    def as_row(col):
        return jnp.sum(eye * col, axis=0, keepdims=True)

    def local_stats(value, i):
        peak = jnp.max(value, axis=1, keepdims=True)
        grown = jnp.exp(value - peak)
        total = jnp.sum(grown, axis=1, keepdims=True)
        stats[i, me_dest, 0:1, 0:rows] = as_row(peak)
        stats[i, me_dest, 1:2, 0:rows] = as_row(total)
        dest[1 + i].share(stats.at[i])
        return grown

    def joint_stats(i):
        dest[1 + i].landed()
        peaks = [stats[i, j, 0:1, 0:rows] for j in range(n_dest)]
        peak = functools.reduce(jnp.maximum, peaks)
        total = jnp.zeros_like(peak)
        for j in range(n_dest):
            total = total + stats[i, j, 1:2, 0:rows] * jnp.exp(peaks[j] - peak)
        return peak, total

    def start_modelled(i, pieces, peak, total):
        scale = jnp.exp(stats[i, me_dest, 0:1, 0:rows] - peak) / total
        left, left_low = halves(worker_hot * scale)
        parts[i, me_orig] = (
            dot(left, pieces[0]) + (dot(left, pieces[1]) + dot(left_low, pieces[0]))
        )
        orig[1 + i].share(parts.at[i])

    def end_modelled(i):
        orig[1 + i].landed()
        out = parts[i, 0]
        for j in range(1, n_orig):
            out = out + parts[i, j]
        return out

    grown = local_stats(base[...], 0)
    pieces = halves(grown)
    dest[0].landed()
    orig[0].landed()
    size_total, seg_total = sizes[0], segs[0]
    for j in range(1, n_dest):
        size_total = size_total + sizes[j]
    for j in range(1, n_orig):
        seg_total = seg_total + segs[j]
    target = size_term * (seg_total / size_total)[:, 0:1] + 1.0
    peak, total = joint_stats(0)
    start_modelled(0, pieces, peak, total)
    shadow = jnp.log(target / (end_modelled(0) + 1.0))

    grown = local_stats(base[...] + by_segment(shadow), 1)
    inv_total[...] = grown * inv_total[...]

    def flow_step(g):
        first = pl.multiple_of(g * GROUP, GROUP)
        mixed = mode_exp[g] * inv_total[pl.ds(first, GROUP), :][None]
        top, low = halves(mixed.reshape(block, zones))
        out = dot_nt(top, dist_hot[...]) + dot_nt(low, dist_hot[...])
        half = block // 2
        flows[pl.ds(pl.multiple_of(g * half, half), half), :] = jnp.concatenate(
            [out[:half], out[half:]], axis=1
        )

    chunk = flow_in.shape[1]

    size = chunk // PIECES

    def piece_of(ref, j, p):
        return ref.at[pl.ds(pl.multiple_of(j * chunk + p * size, size), size)]

    def send_flows(p, steps):
        dest[3 + p].start(
            lambda peer: piece_of(flows, peer, p),
            lambda mine: flow_in.at[mine, pl.ds(p * size, size)],
            steps,
        )

    early = n_dest == groups
    for i in range(groups):
        flow_step(lax.rem(me_dest + 1 + i, groups))
        if early and i + 1 < n_dest:
            send_flows(0, [i + 1])
    for p in range(1 if early else 0, PIECES):
        send_flows(p, range(1, n_dest))
    pieces = halves(grown)
    peak, total = joint_stats(1)
    start_modelled(1, pieces, peak, total)
    access_out[...] = peak + jnp.log(total)
    flow_in[me_dest] = flows[pl.ds(pl.multiple_of(me_dest * chunk, chunk), chunk), :]
    span = block // 2
    scales = [
        jnp.exp(stats[1, j, 0:1, 0:rows] - peak) / total * workers[...] for j in range(n_dest)
    ]
    for p in range(PIECES):
        flat = iota((size, rows), 0) + (me_dest * chunk + p * size)
        pick = hot(iota((size, rows), 1) == flat // span * GROUP + flat % GROUP)
        weight = [jnp.sum(pick * scale, axis=1, keepdims=True) for scale in scales]
        dest[3 + p].landed()
        reduced = jnp.zeros((size, flows.shape[1]), F32)
        for j in range(n_dest):
            reduced = reduced + flow_in[j, p * size : (p + 1) * size] * weight[j]
        flow_out[pl.ds(pl.multiple_of(me_dest * chunk + p * size, size), size), :] = reduced
        dest[3 + PIECES + p].start(
            lambda peer: piece_of(flow_out, me_dest, p),
            lambda mine: piece_of(flow_out, mine, p),
        )
    modelled = end_modelled(1)
    modelled_out[...] = modelled
    shadow_out[...] = shadow + jnp.log(target / (modelled + 1.0))
    for p in range(PIECES):
        dest[3 + PIECES + p].landed()
    for one in dest + orig:
        one.sent()


def finish(
    mode_count, groups, flow, access, modelled, shadow, flow_out, access_out,
    modelled_out, shadow_out, table, spread, sem, table_sem,
):
    copies = [
        pltpu.make_async_copy(a, b, sem.at[i])
        for i, (a, b) in enumerate(
            ((access, access_out), (modelled, modelled_out), (shadow, shadow_out))
        )
    ]
    for copy in copies:
        copy.start()
    lanes = flow.shape[1]
    half = mode_count // 2
    rows = groups * GROUP
    width = table.shape[1]
    source = iota((2 * lanes, 1), 0)
    place = source % (lanes // 2) * mode_count + source // lanes
    place = place + source % lanes // (lanes // 2) * half
    starts = [(t, m) for t in range(0, width, TILE) for m in range(0, half, 2)]
    for i, (t, m) in enumerate(starts):
        spread[i] = hot(iota((2 * lanes, TILE), 1) == place + (m - t), BF16)
    pieces = flow[...].reshape(groups, half, GROUP, lanes)
    pairs = []
    for m in range(0, half, 2):
        pair = [pieces[:, m + i].reshape(rows, lanes) for i in range(2)]
        pairs.append(jnp.concatenate(halves(jnp.concatenate(pair, axis=1)), axis=0))
    for t in range(0, width, TILE):
        total = jnp.zeros((2 * rows, TILE), F32)
        for i, (start, m) in enumerate(starts):
            if start == t:
                total = total + dot(pairs[m // 2], spread[i])
        cols = slice(t, t + TILE)
        table[:, cols] = total[:rows] + total[rows:]
        copy = pltpu.make_async_copy(
            table.at[:, cols], flow_out.at[:, cols], table_sem.at[t // TILE]
        )
        copy.start()
        copies.append(copy)
    for copy in copies:
        copy.wait()


def per_device(
    n_dest,
    n_orig,
    skims,
    coef,
    asc,
    theta,
    beta,
    employment,
    zone_district,
    anchor_district,
    district_const,
    segment,
    availability,
    workers,
):
    skim_count, rows, zones = skims.shape
    seg_count = theta.shape[0]
    mode_count = availability.shape[1]
    dist_count = district_const.shape[0]
    groups = rows // GROUP
    inputs = (
        skims,
        coef.T,
        asc.reshape(1, -1),
        theta.reshape(1, -1),
        beta,
        employment,
        zone_district.reshape(1, -1),
        anchor_district.reshape(1, -1),
        district_const,
        segment.reshape(1, -1),
        availability.T,
        workers.reshape(1, -1),
    )
    flow_rows = rows * mode_count // 2
    chunk = flow_rows // n_dest
    lanes = max(128, rows)
    vmem = pl.BlockSpec(memory_space=pltpu.VMEM)
    sem = pltpu.SemaphoreType.DMA
    access, flow, modelled, shadow = pl.pallas_call(
        functools.partial(kernel, n_dest, n_orig),
        out_shape=(
            pltpu.VMEM((1, rows), F32),
            pltpu.VMEM((flow_rows, 2 * dist_count), F32),
            pltpu.VMEM((seg_count, zones), F32),
            pltpu.VMEM((seg_count, zones), F32),
        ),
        in_specs=[pl.BlockSpec(memory_space=pl.ANY)] * 12,
        out_specs=(vmem,) * 4,
        scratch_shapes=[pltpu.VMEM(x.shape, x.dtype) for x in inputs]
        + [
            pltpu.VMEM((groups, mode_count, GROUP, zones), F32),
            pltpu.VMEM((rows, zones), F32),
            pltpu.VMEM((rows * mode_count, skims.shape[0] * GROUP), BF16),
            pltpu.VMEM((rows * mode_count, 128), F32),
            pltpu.VMEM((rows, 128), F32),
            pltpu.VMEM((rows, zones), F32),
            pltpu.VMEM((dist_count, zones), BF16),
            pltpu.VMEM((n_dest, seg_count, 128), F32),
            pltpu.VMEM((n_orig, seg_count, 128), F32),
            pltpu.VMEM((2, n_dest, 8, lanes), F32),
            pltpu.VMEM((2, n_orig, seg_count, zones), F32),
            pltpu.VMEM((flow_rows, 2 * dist_count), F32),
            pltpu.VMEM((n_dest, chunk, 2 * dist_count), F32),
            sem((3 + 2 * PIECES, n_dest - 1)),
            sem((3 + 2 * PIECES, n_dest - 1)),
            sem((3, n_orig - 1)),
            sem((3, n_orig - 1)),
            sem((groups,)),
            sem((len(inputs) - 1,)),
        ],
        compiler_params=pltpu.CompilerParams(
            collective_id=0, has_side_effects=True, vmem_limit_bytes=33554432
        ),
    )(*(pltpu.with_memory_space_constraint(x, pltpu.HBM) for x in inputs))
    anywhere = pl.BlockSpec(memory_space=pl.ANY)
    width = dist_count * mode_count
    results = [pltpu.with_memory_space_constraint(x, pltpu.VMEM) for x in (flow, access, modelled, shadow)]
    flow, access, modelled, shadow = pl.pallas_call(
        functools.partial(finish, mode_count, groups),
        out_shape=(jax.ShapeDtypeStruct((rows, dist_count * mode_count), F32),)
        + tuple(jax.ShapeDtypeStruct(x.shape, x.dtype) for x in results[1:]),
        in_specs=[vmem] * 4,
        out_specs=(anywhere,) * 4,
        scratch_shapes=[
            pltpu.VMEM((rows, width), F32),
            pltpu.VMEM((width // TILE * (mode_count // 4), 4 * dist_count, TILE), BF16),
            sem((3,)),
            sem((width // TILE,)),
        ],
        compiler_params=pltpu.CompilerParams(vmem_limit_bytes=16777216),
    )(*results)
    return access.reshape(rows), flow, modelled, shadow


def solution(mesh):
    return jax.shard_map(
        functools.partial(per_device, mesh.shape["dest"], mesh.shape["orig"]),
        mesh=mesh,
        in_specs=(
            P(None, ("scen", "orig"), "dest"),
            P(),
            P(),
            P(),
            P(),
            P(None, ("scen", "dest")),
            P("dest"),
            P(("scen", "orig")),
            P(),
            P(("scen", "orig")),
            P(("scen", "orig"), None),
            P(("scen", "orig")),
        ),
        out_specs=(
            P(("scen", "orig")),
            P(("scen", "orig"), None),
            P(None, ("scen", "dest")),
            P(None, ("scen", "dest")),
        ),
        check_vma=False,
    )
```

```python
import functools

import jax
import jax.numpy as jnp
from jax import lax
from jax.experimental import pallas as pl
from jax.experimental.pallas import tpu as pltpu
from jax.sharding import PartitionSpec as P

HIGH = lax.Precision.HIGHEST
F32 = jnp.float32
BF16 = jnp.bfloat16
MESH = pl.DeviceIdType.MESH
GROUP = 16
TILE = 256
PIECES = 2
LAG = 4
LEAD = 2
WAIT = 2


def iota(shape, dim):
    return lax.broadcasted_iota(jnp.int32, shape, dim)


def hot(mask, dtype=F32):
    return jnp.where(mask, 1.0, 0.0).astype(dtype)


def dot(a, b, precision=None):
    return jnp.dot(a, b, preferred_element_type=F32, precision=precision)


def dot_nt(a, b):
    return lax.dot_general(a, b, (((1,), (1,)), ((), ())), preferred_element_type=F32)


def halves(x):
    top = x.astype(BF16)
    return top, (x - top.astype(F32)).astype(BF16)


class Exchange:
    def __init__(self, axis, count, send_sem, recv_sem, buf):
        self.axis, self.count, self.buf = axis, count, buf
        self.send_sem, self.recv_sem = send_sem, recv_sem

    def copies(self):
        me = lax.axis_index(self.axis)
        return [
            pltpu.make_async_remote_copy(
                src_ref=self.buf.at[me],
                dst_ref=self.buf.at[me],
                send_sem=self.send_sem.at[k - 1],
                recv_sem=self.recv_sem.at[k - 1],
                device_id={self.axis: lax.rem(me + k, self.count)},
                device_id_type=MESH,
            )
            for k in range(1, self.count)
        ]

    def share(self):
        for copy in self.copies():
            copy.start()

    def landed(self):
        for copy in self.copies():
            copy.wait_recv()

    def sent(self):
        for copy in self.copies():
            copy.wait_send()


def kernel(
    n_dest,
    n_orig,
    skims_hbm,
    coef_hbm,
    asc_hbm,
    theta_hbm,
    beta_hbm,
    employment_hbm,
    zone_district_hbm,
    anchor_district_hbm,
    district_const_hbm,
    segment_hbm,
    availability_hbm,
    workers_hbm,
    access_out,
    flow_out,
    modelled_out,
    shadow_out,
    scale_rows,
    skims,
    coef,
    asc,
    theta,
    beta,
    employment,
    zone_district,
    anchor_district,
    district_const,
    segment,
    availability,
    workers,
    mode_exp,
    inv_total,
    weights,
    added,
    theta_rows,
    base,
    dist_hot,
    sizes,
    segs,
    stats,
    parts,
    flows,
    inbox,
    turned,
    carry,
    ahead,
    dest_send,
    dest_recv,
    orig_send,
    orig_recv,
    sum_send,
    sum_recv,
    back_send,
    back_recv,
    turn_send,
    skim_sem,
    load_sem,
):
    skim_count, rows, zones = skims.shape
    seg_count = theta.shape[1]
    mode_count = availability.shape[0]
    dist_count = district_const.shape[0]
    groups = rows // GROUP
    me_dest = lax.axis_index("dest")
    me_orig = lax.axis_index("orig")
    dest = [
        Exchange("dest", n_dest, dest_send.at[i], dest_recv.at[i], buf)
        for i, buf in enumerate((sizes, stats.at[0], stats.at[1]))
    ]
    orig = [
        Exchange("orig", n_orig, orig_send.at[i], orig_recv.at[i], buf)
        for i, buf in enumerate((segs, parts.at[0], parts.at[1]))
    ]

    barrier = pltpu.get_barrier_semaphore()
    for axis, me, count in (("dest", me_dest, n_dest), ("orig", me_orig, n_orig)):
        for k in range(1, count):
            pl.semaphore_signal(
                barrier,
                inc=1,
                device_id={axis: lax.rem(me + k, count)},
                device_id_type=MESH,
            )
    small = [
        (segment_hbm, segment),
        (workers_hbm, workers),
        (beta_hbm, beta),
        (employment_hbm, employment),
        (zone_district_hbm, zone_district),
        (coef_hbm, coef),
        (asc_hbm, asc),
        (availability_hbm, availability),
        (theta_hbm, theta),
        (anchor_district_hbm, anchor_district),
        (district_const_hbm, district_const),
    ]
    loads = [pltpu.make_async_copy(a, b, load_sem.at[i]) for i, (a, b) in enumerate(small)]

    def skim_load(g):
        part = pl.ds(pl.multiple_of(g * GROUP, GROUP), GROUP)
        return pltpu.make_async_copy(skims_hbm.at[:, part], skims.at[:, part], skim_sem.at[g])

    for load in loads:
        load.start()
    for g in range(groups):
        skim_load(g).start()
    for load in loads:
        load.wait()

    seg_hot_t = hot(segment[...] == iota((seg_count, rows), 0))
    worker_hot = seg_hot_t * workers[...]
    eye = hot(iota((rows, rows), 0) == iota((rows, rows), 1))
    seg_hot = dot_nt(eye.astype(BF16), seg_hot_t.astype(BF16))
    size_term = jnp.zeros((seg_count, zones), F32)
    for c in range(beta.shape[1]):
        size_term = size_term + beta[:, c : c + 1] * employment[c : c + 1, :].astype(F32)
    sizes[me_dest] = jnp.broadcast_to(jnp.sum(size_term, axis=1, keepdims=True), sizes.shape[1:])
    segs[me_orig] = jnp.broadcast_to(jnp.sum(worker_hot, axis=1, keepdims=True), segs.shape[1:])
    dist_hot[...] = hot(zone_district[...] == iota((dist_count, zones), 0), BF16)

    def by_segment(table):
        out = jnp.zeros((rows, table.shape[1]), F32)
        for s in range(seg_count):
            out = jnp.where(seg_hot[:, s : s + 1] > 0.5, table[s : s + 1, :], out)
        return out

    theta_rows[...] = jnp.broadcast_to(
        jnp.sum(seg_hot * theta[...], axis=1, keepdims=True), theta_rows.shape
    )
    anchor_hot_t = hot(anchor_district[...] == iota((dist_count, rows), 0), BF16)
    anchor_hot = dot_nt(eye.astype(BF16), anchor_hot_t)
    anchor_const = dot(anchor_hot, district_const[...], HIGH)
    top, low = halves(anchor_const)
    rest = (anchor_const - top.astype(F32) - low.astype(F32)).astype(BF16)
    pair_const = dot(jnp.concatenate([top, low, rest], axis=0), dist_hot[...])
    pair_const = pair_const[:rows] + (pair_const[rows : 2 * rows] + pair_const[2 * rows :])
    base[...] = by_segment(jnp.log(size_term)) + pair_const

    block = mode_count * GROUP
    width = skim_count * GROUP
    row = iota((groups * block, 1), 0)
    row_mode, row_anchor = row % block // GROUP, row % GROUP
    pair = seg_count * mode_count
    spread = hot(iota((seg_count, pair), 1) // mode_count == iota((seg_count, pair), 0), BF16)
    widen = hot(iota((skim_count, width), 1) // GROUP == iota((skim_count, width), 0), BF16)
    pick = hot(iota((groups * block, rows), 1) == row // block * GROUP + row_anchor, BF16)
    row_seg = dot_nt(pick, seg_hot_t.astype(BF16)).astype(BF16)
    mode_match = iota((groups * block, pair), 1) % mode_count == row_mode
    row_pair = jnp.where(mode_match, dot(row_seg, spread), 0.0)
    row_asc = jnp.sum(row_pair * asc[...], axis=1, keepdims=True)
    row_coef = dot_nt(row_pair.astype(BF16), coef[...]).astype(BF16)
    anchor_match = iota((groups * block, width), 1) % GROUP == row_anchor
    weights[...] = jnp.where(anchor_match, dot(row_coef, widen), 0.0).astype(BF16)
    open_modes = dot_nt(pick, hot(availability[...] > 0, BF16))
    own_mode = iota((groups * block, mode_count), 1) == row_mode
    usable = jnp.sum(jnp.where(own_mode, open_modes, 0.0), axis=1, keepdims=True)
    usable = usable + hot(row_mode == 0)
    added[...] = jnp.broadcast_to(
        row_asc + jnp.where(usable > 0.5, 0.0, -1e30), added.shape
    )

    def group_step(g, carry):
        first = pl.multiple_of(g * GROUP, GROUP)
        skim_load(g).wait()
        mine = pl.ds(pl.multiple_of(g * block, block), block)
        theta_col = theta_rows[pl.ds(first, GROUP), 0:1]
        for t in range(zones // TILE):
            cols = slice(t * TILE, (t + 1) * TILE)
            near = skims[:, pl.ds(first, GROUP), cols].reshape(width, TILE)
            utility = (dot(weights[mine, :], near) + added[mine, 0:1]).reshape(mode_count, GROUP, TILE)
            peak = jnp.max(utility, axis=0)
            grown = jnp.exp(utility - peak[None])
            total = jnp.sum(grown, axis=0)
            mode_exp[g, :, :, cols] = grown
            inv_total[pl.ds(first, GROUP), cols] = 1.0 / total
            base[pl.ds(first, GROUP), cols] += theta_col * (peak + jnp.log(total))
        return carry

    lax.fori_loop(0, groups, group_step, 0, unroll=True)

    pl.semaphore_wait(barrier, n_dest + n_orig - 2)
    dest[0].share()
    orig[0].share()

    def as_row(col):
        return jnp.sum(eye * col, axis=0, keepdims=True)

    def local_stats(value):
        peak = jnp.max(value, axis=1, keepdims=True)
        grown = jnp.exp(value - peak)
        total = jnp.sum(grown, axis=1, keepdims=True)
        stats[0, me_dest, 0:1, 0:rows] = as_row(peak)
        stats[0, me_dest, 1:2, 0:rows] = as_row(total)
        dest[1].share()
        return grown, peak

    def start_modelled(i, pieces, scale):
        left, left_low = halves(worker_hot * scale)
        parts[i, me_orig] = (
            dot(left, pieces[0]) + (dot(left, pieces[1]) + dot(left_low, pieces[0]))
        )
        orig[1 + i].share()

    def end_modelled(i):
        orig[1 + i].landed()
        out = parts[i, 0]
        for j in range(1, n_orig):
            out = out + parts[i, j]
        return out

    grown, local_peak = local_stats(base[...])
    pieces = halves(grown)
    dest[0].landed()
    orig[0].landed()
    size_total, seg_total = sizes[0], segs[0]
    for j in range(1, n_dest):
        size_total = size_total + sizes[j]
    for j in range(1, n_orig):
        seg_total = seg_total + segs[j]
    target = size_term * (seg_total / size_total)[:, 0:1] + 1.0
    dest[1].landed()
    peaks = [stats[0, j, 0:1, 0:rows] for j in range(n_dest)]
    peak = functools.reduce(jnp.maximum, peaks)
    total = jnp.zeros_like(peak)
    for j in range(n_dest):
        total = total + stats[0, j, 1:2, 0:rows] * jnp.exp(peaks[j] - peak)
    start_modelled(0, pieces, jnp.exp(stats[0, me_dest, 0:1, 0:rows] - peak) / total)
    joint_peak = jnp.sum(eye * peak, axis=1, keepdims=True)
    grown = grown * jnp.exp(local_peak - joint_peak)
    base[...] = grown * inv_total[...]
    ratio = target / (end_modelled(0) + 1.0)
    ratio_rows = by_segment(ratio)
    grown = grown * ratio_rows
    base[...] = base[...] * ratio_rows
    stats[1, me_dest, 0:1, 0:rows] = as_row(jnp.sum(grown, axis=1, keepdims=True))
    dest[2].share()

    half = mode_count // 2
    span = half // PIECES
    chunks = groups * PIECES
    size = span * GROUP
    middle = n_dest // 2
    odd = lax.rem(me_orig, 2) == 1
    inward = jnp.where(me_dest < middle, 1, -1)
    inner = jnp.logical_or(me_dest == middle - 1, me_dest == middle)
    outer = jnp.logical_and(me_dest != 0, me_dest != n_dest - 1)
    lane = jnp.where(inner, 1, 0)
    toward = me_dest + inward
    away = jnp.where(outer, me_dest - inward, toward)

    def rows_of(ref, c):
        return ref.at[pl.ds(pl.multiple_of(c * size, size), size)]

    def copy_in(c, slot, place, device, source=flows):
        return pltpu.make_async_remote_copy(
            src_ref=rows_of(source, c),
            dst_ref=rows_of(inbox.at[slot], place),
            send_sem=sum_send.at[c],
            recv_sem=sum_recv.at[slot, place],
            device_id=device,
            device_id_type=MESH,
        )

    def sum_copy(c, slot, source=flows):
        return copy_in(c, n_dest + slot, c, {"dest": toward}, source)

    def give_copy(c, source):
        return copy_in(c, source, c // 2, {"dest": middle - 1 + c % 2})

    def first_copy(c):
        return copy_in(
            c,
            jnp.where(odd, n_dest + lane, me_dest),
            jnp.where(odd, c, c // 2),
            {"dest": jnp.where(odd, toward, middle - 1 + c % 2)},
        )

    def back_copy(c):
        return pltpu.make_async_remote_copy(
            src_ref=rows_of(flow_out, c),
            dst_ref=rows_of(flow_out, c),
            send_sem=back_send.at[c],
            recv_sem=back_recv.at[c],
            device_id={"dest": away},
            device_id_type=MESH,
        )

    def other(i):
        return i + jnp.where(i >= me_dest, 1, 0)

    def turn_copy(k, i):
        c = 2 * k + me_dest - (middle - 1)
        return pltpu.make_async_remote_copy(
            src_ref=rows_of(flow_out, c),
            dst_ref=rows_of(flow_out, c),
            send_sem=turn_send.at[k, i],
            recv_sem=back_recv.at[c],
            device_id={"dest": other(i)},
            device_id_type=MESH,
        )

    def own_chunk(c):
        g, p = c // PIECES, c % PIECES
        factor = base[g * GROUP : (g + 1) * GROUP, :][None]
        mixed = jnp.concatenate(
            [
                mode_exp[g, k + p * span : k + (p + 1) * span] * factor
                for k in (0, half)
            ],
            axis=0,
        )
        top, low = halves(mixed.reshape(2 * size, zones))
        out = dot_nt(top, dist_hot[...]) + dot_nt(low, dist_hot[...])
        flows[c * size : (c + 1) * size, :] = jnp.concatenate([out[:size], out[size:]], axis=1)

    def joint_total():
        dest[2].landed()
        total = stats[1, 0, 0:1, 0:rows]
        for j in range(1, n_dest):
            total = total + stats[1, j, 0:1, 0:rows]
        start_modelled(1, halves(grown), 1.0 / total)
        access_out[...] = peak + jnp.log(total)
        scale = jnp.sum(eye * (workers[...] / total), axis=1, keepdims=True)
        scale_rows[...] = jnp.broadcast_to(scale, scale_rows.shape)

    def at(c):
        return slice(c * size, (c + 1) * size)

    def gather(c):
        sum_copy(c, 0).wait_recv()
        carry[at(c), :] = flows[at(c), :] + inbox[n_dest, at(c), :]
        sum_copy(c, lane, carry).start()

    def turn(c):
        sum_copy(c, 1).wait_recv()
        flow_out[at(c), :] = carry[at(c), :] + inbox[n_dest + 1, at(c), :]
        back_copy(c).start()

    def ahead_copy(c):
        return pltpu.make_async_remote_copy(
            src_ref=rows_of(ahead, c),
            dst_ref=rows_of(inbox.at[n_dest], c),
            send_sem=back_send.at[c],
            recv_sem=back_recv.at[c],
            device_id={"dest": 0},
            device_id_type=MESH,
        )

    def send_ahead(c):
        sum_copy(c, 1).wait_recv()
        ahead[at(c), :] = flows[at(c), :] + inbox[n_dest + 1, at(c), :]
        ahead_copy(c).start()

    def place_of(k):
        c = 2 * k + me_dest - (middle - 1)
        return pl.ds(pl.multiple_of(c * size, size), size)

    def early_copy(k):
        c = 2 * k + me_dest - (middle - 1)
        return pltpu.make_async_remote_copy(
            src_ref=rows_of(turned, k),
            dst_ref=rows_of(inbox.at[0], c),
            send_sem=turn_send.at[k, 0],
            recv_sem=back_recv.at[c],
            device_id={"dest": 0},
            device_id_type=MESH,
        )

    def serve(k):
        for i in range(1, n_dest - 1):
            give_copy(2 * k, other(i)).wait_recv()
        both = flows[place_of(k), :]
        for i in range(1, n_dest - 1):
            both = both + inbox[other(i), at(k), :]
        turned[at(k), :] = both
        early_copy(k).start()

    def serve_rest(k):
        give_copy(2 * k, 0).wait_recv()
        flow_out[place_of(k), :] = turned[at(k), :] + inbox[0, at(k), :]
        for i in range(1, n_dest - 1):
            turn_copy(k, i).start()

    line_mid = jnp.logical_and(odd, outer)
    serves = jnp.logical_and(jnp.logical_not(odd), inner)
    short = jnp.int32(middle) == 2
    adds = jnp.logical_and(me_dest == 0, jnp.logical_or(jnp.logical_not(odd), short))
    plain = jnp.logical_not(jnp.logical_or(line_mid, serves))

    def not_mine(c):
        return me_dest != middle - 1 + c % 2

    @pl.when(line_mid)
    def _():
        for c in range(chunks):
            own_chunk(c)

    @pl.when(serves)
    def _():
        for c in range(chunks):
            own_chunk(c)
            pl.when(not_mine(c))(lambda c=c: first_copy(c).start())

        for k in range(chunks // 2):
            if k == WAIT:
                joint_total()
            serve(k)
        for k in range(chunks // 2):
            serve_rest(k)

    @pl.when(plain)
    def _():
        for c in range(chunks):
            own_chunk(c)
            first_copy(c).start()

    line_inner = jnp.logical_and(odd, inner)

    leads = jnp.logical_and(line_inner, jnp.logical_and(short, me_dest == 1))

    @pl.when(leads)
    def _():
        for c in range(chunks + LEAD):
            if c == WAIT:
                joint_total()
            if c < chunks:
                gather(c)
            if c >= LEAD:
                send_ahead(c - LEAD)
        flow_out[...] = carry[...] + inbox[n_dest + 1]

    @pl.when(jnp.logical_and(line_inner, jnp.logical_not(leads)))
    def _():
        for c in range(chunks + LAG):
            if c == WAIT:
                joint_total()
            if c < chunks:
                gather(c)
            if c >= LAG:
                turn(c - LAG)

    @pl.when(jnp.logical_not(inner))
    def _():
        joint_total()

        @pl.when(line_mid)
        def _():
            for c in range(chunks):
                gather(c)

    modelled = end_modelled(1)
    modelled_out[...] = modelled
    shadow_out[...] = jnp.log(ratio) + jnp.log(target / (modelled + 1.0))

    @pl.when(jnp.logical_not(jnp.logical_or(line_inner, serves)))
    def _():
        for c in range(chunks):
            back_copy(c).wait_recv()

            @pl.when(line_mid)
            def _():
                back_copy(c).start()

            @pl.when(adds)
            def _():
                flow_out[at(c), :] = flows[at(c), :] + inbox[jnp.where(odd, n_dest, 0), at(c), :]

    @pl.when(serves)
    def _():
        for c in range(chunks):

            @pl.when(not_mine(c))
            def _():
                back_copy(c).wait_recv()
                sum_copy(c, lane).wait_send()

        for k in range(chunks // 2):
            for i in range(n_dest - 1):
                turn_copy(k, i).wait_send()

    @pl.when(jnp.logical_not(serves))
    def _():
        for c in range(chunks):
            sum_copy(c, lane).wait_send()

    @pl.when(line_mid)
    def _():
        for c in range(chunks):
            back_copy(c).wait_send()

    for one in dest + orig:
        one.sent()


def finish(
    mode_count, groups, flow, access, modelled, shadow, scale, flow_out, access_out,
    modelled_out, shadow_out, table, spread, sem, table_sem,
):
    copies = [
        pltpu.make_async_copy(a, b, sem.at[i])
        for i, (a, b) in enumerate(
            ((access, access_out), (modelled, modelled_out), (shadow, shadow_out))
        )
    ]
    for copy in copies:
        copy.start()
    lanes = flow.shape[1]
    half = mode_count // 2
    rows = groups * GROUP
    width = table.shape[1]
    source = iota((2 * lanes, 1), 0)
    place = source % (lanes // 2) * mode_count + source // lanes
    place = place + source % lanes // (lanes // 2) * half
    starts = [(t, m) for t in range(0, width, TILE) for m in range(0, half, 2)]
    for i, (t, m) in enumerate(starts):
        spread[i] = hot(iota((2 * lanes, TILE), 1) == place + (m - t), BF16)
    pieces = flow[...].reshape(groups, half, GROUP, lanes)
    pieces = pieces * scale[...].reshape(groups, 1, GROUP, lanes)
    pairs = []
    for m in range(0, half, 2):
        pair = [pieces[:, m + i].reshape(rows, lanes) for i in range(2)]
        pairs.append(jnp.concatenate(halves(jnp.concatenate(pair, axis=1)), axis=0))
    for t in range(0, width, TILE):
        total = jnp.zeros((2 * rows, TILE), F32)
        for i, (start, m) in enumerate(starts):
            if start == t:
                total = total + dot(pairs[m // 2], spread[i])
        cols = slice(t, t + TILE)
        table[:, cols] = total[:rows] + total[rows:]
        copy = pltpu.make_async_copy(
            table.at[:, cols], flow_out.at[:, cols], table_sem.at[t // TILE]
        )
        copy.start()
        copies.append(copy)
    for copy in copies:
        copy.wait()


def per_device(
    n_dest,
    n_orig,
    skims,
    coef,
    asc,
    theta,
    beta,
    employment,
    zone_district,
    anchor_district,
    district_const,
    segment,
    availability,
    workers,
):
    skim_count, rows, zones = skims.shape
    seg_count = theta.shape[0]
    mode_count = availability.shape[1]
    dist_count = district_const.shape[0]
    groups = rows // GROUP
    inputs = (
        skims,
        coef.T,
        asc.reshape(1, -1),
        theta.reshape(1, -1),
        beta,
        employment,
        zone_district.reshape(1, -1),
        anchor_district.reshape(1, -1),
        district_const,
        segment.reshape(1, -1),
        availability.T,
        workers.reshape(1, -1),
    )
    flow_rows = rows * mode_count // 2
    lanes = max(128, rows)
    chunks = groups * PIECES
    vmem = pl.BlockSpec(memory_space=pltpu.VMEM)
    sem = pltpu.SemaphoreType.DMA
    access, flow, modelled, shadow, scale = pl.pallas_call(
        functools.partial(kernel, n_dest, n_orig),
        out_shape=(
            pltpu.VMEM((1, rows), F32),
            pltpu.VMEM((flow_rows, 2 * dist_count), F32),
            pltpu.VMEM((seg_count, zones), F32),
            pltpu.VMEM((seg_count, zones), F32),
            pltpu.VMEM((rows, 2 * dist_count), F32),
        ),
        in_specs=[pl.BlockSpec(memory_space=pl.ANY)] * 12,
        out_specs=(vmem,) * 5,
        scratch_shapes=[pltpu.VMEM(x.shape, x.dtype) for x in inputs]
        + [
            pltpu.VMEM((groups, mode_count, GROUP, zones), F32),
            pltpu.VMEM((rows, zones), F32),
            pltpu.VMEM((rows * mode_count, skims.shape[0] * GROUP), BF16),
            pltpu.VMEM((rows * mode_count, 128), F32),
            pltpu.VMEM((rows, 128), F32),
            pltpu.VMEM((rows, zones), F32),
            pltpu.VMEM((dist_count, zones), BF16),
            pltpu.VMEM((n_dest, seg_count, 128), F32),
            pltpu.VMEM((n_orig, seg_count, 128), F32),
            pltpu.VMEM((2, n_dest, 8, lanes), F32),
            pltpu.VMEM((2, n_orig, seg_count, zones), F32),
            pltpu.VMEM((flow_rows, 2 * dist_count), F32),
            pltpu.VMEM((n_dest + 2, flow_rows, 2 * dist_count), F32),
            pltpu.VMEM((flow_rows // 2, 2 * dist_count), F32),
            pltpu.VMEM((flow_rows, 2 * dist_count), F32),
            pltpu.VMEM((flow_rows, 2 * dist_count), F32),
            sem((3, n_dest - 1)),
            sem((3, n_dest - 1)),
            sem((3, n_orig - 1)),
            sem((3, n_orig - 1)),
            sem((chunks,)),
            sem((n_dest + 2, chunks)),
            sem((chunks,)),
            sem((chunks,)),
            sem((chunks // 2, n_dest - 1)),
            sem((groups,)),
            sem((len(inputs) - 1,)),
        ],
        compiler_params=pltpu.CompilerParams(
            collective_id=0, has_side_effects=True, vmem_limit_bytes=33554432
        ),
    )(*(pltpu.with_memory_space_constraint(x, pltpu.HBM) for x in inputs))
    anywhere = pl.BlockSpec(memory_space=pl.ANY)
    width = dist_count * mode_count
    results = [
        pltpu.with_memory_space_constraint(x, pltpu.VMEM)
        for x in (flow, access, modelled, shadow, scale)
    ]
    flow, access, modelled, shadow = pl.pallas_call(
        functools.partial(finish, mode_count, groups),
        out_shape=(jax.ShapeDtypeStruct((rows, dist_count * mode_count), F32),)
        + tuple(jax.ShapeDtypeStruct(x.shape, x.dtype) for x in results[1:4]),
        in_specs=[vmem] * 5,
        out_specs=(anywhere,) * 4,
        scratch_shapes=[
            pltpu.VMEM((rows, width), F32),
            pltpu.VMEM((width // TILE * (mode_count // 4), 4 * dist_count, TILE), BF16),
            sem((3,)),
            sem((width // TILE,)),
        ],
        compiler_params=pltpu.CompilerParams(vmem_limit_bytes=16777216),
    )(*results)
    return access.reshape(rows), flow, modelled, shadow


def solution(mesh):
    return jax.shard_map(
        functools.partial(per_device, mesh.shape["dest"], mesh.shape["orig"]),
        mesh=mesh,
        in_specs=(
            P(None, ("scen", "orig"), "dest"),
            P(),
            P(),
            P(),
            P(),
            P(None, ("scen", "dest")),
            P("dest"),
            P(("scen", "orig")),
            P(),
            P(("scen", "orig")),
            P(("scen", "orig"), None),
            P(("scen", "orig")),
        ),
        out_specs=(
            P(("scen", "orig")),
            P(("scen", "orig"), None),
            P(None, ("scen", "dest")),
            P(None, ("scen", "dest")),
        ),
        check_vma=False,
    )
```

```python
import functools

import jax
import jax.numpy as jnp
from jax import lax
from jax.experimental import pallas as pl
from jax.experimental.pallas import tpu as pltpu
from jax.sharding import PartitionSpec as P

HIGH = lax.Precision.HIGHEST
F32 = jnp.float32
BF16 = jnp.bfloat16
MESH = pl.DeviceIdType.MESH
GROUP = 16
TILE = 256
PIECES = 2
LAG = 4
LEAD = 2
WAIT = 2


def iota(shape, dim):
    return lax.broadcasted_iota(jnp.int32, shape, dim)


def hot(mask, dtype=F32):
    return jnp.where(mask, 1.0, 0.0).astype(dtype)


def dot(a, b, precision=None):
    return jnp.dot(a, b, preferred_element_type=F32, precision=precision)


def dot_nt(a, b):
    return lax.dot_general(a, b, (((1,), (1,)), ((), ())), preferred_element_type=F32)


def halves(x):
    top = x.astype(BF16)
    return top, (x - top.astype(F32)).astype(BF16)


class Exchange:
    def __init__(self, axis, count, send_sem, recv_sem, buf):
        self.axis, self.count, self.buf = axis, count, buf
        self.send_sem, self.recv_sem = send_sem, recv_sem

    def copy(self, part, k):
        me = lax.axis_index(self.axis)
        return pltpu.make_async_remote_copy(
            src_ref=self.buf.at[part],
            dst_ref=self.buf.at[part],
            send_sem=self.send_sem,
            recv_sem=self.recv_sem,
            device_id={self.axis: lax.rem(me + k, self.count)},
            device_id_type=MESH,
        )

    def share(self):
        for k in range(1, self.count):
            self.copy(lax.axis_index(self.axis), k).start()

    def landed(self):
        self.copy(pl.ds(0, self.count - 1), 1).wait_recv()

    def sent(self):
        self.copy(pl.ds(0, self.count - 1), 1).wait_send()


def kernel(
    n_dest,
    n_orig,
    skims_hbm,
    coef_hbm,
    asc_hbm,
    theta_hbm,
    beta_hbm,
    employment_hbm,
    zone_district_hbm,
    anchor_district_hbm,
    district_const_hbm,
    segment_hbm,
    availability_hbm,
    workers_hbm,
    access_out,
    flow_out,
    modelled_out,
    shadow_out,
    scale_rows,
    skims,
    coef,
    asc,
    theta,
    beta,
    employment,
    zone_district,
    anchor_district,
    district_const,
    segment,
    availability,
    workers,
    mode_exp,
    inv_total,
    weights,
    theta_rows,
    base,
    dist_hot,
    sizes,
    segs,
    stats,
    parts,
    flows,
    inbox,
    turned,
    carry,
    ahead,
    dest_send,
    dest_recv,
    orig_send,
    orig_recv,
    sum_send,
    sum_recv,
    back_send,
    back_recv,
    turn_send,
    skim_sem,
    load_sem,
):
    skim_count, rows, zones = skims.shape
    seg_count = theta.shape[1]
    mode_count = availability.shape[0]
    dist_count = district_const.shape[0]
    groups = rows // GROUP
    me_dest = lax.axis_index("dest")
    me_orig = lax.axis_index("orig")
    dest = [
        Exchange("dest", n_dest, dest_send.at[i], dest_recv.at[i], buf)
        for i, buf in enumerate((sizes, stats.at[0], stats.at[1]))
    ]
    orig = [
        Exchange("orig", n_orig, orig_send.at[i], orig_recv.at[i], buf)
        for i, buf in enumerate((segs, parts.at[0], parts.at[1]))
    ]

    barrier = pltpu.get_barrier_semaphore()
    for axis, me, count in (("dest", me_dest, n_dest), ("orig", me_orig, n_orig)):
        for k in range(1, count):
            pl.semaphore_signal(
                barrier,
                inc=1,
                device_id={axis: lax.rem(me + k, count)},
                device_id_type=MESH,
            )
    small = [
        (segment_hbm, segment),
        (workers_hbm, workers),
        (beta_hbm, beta),
        (employment_hbm, employment),
        (zone_district_hbm, zone_district),
        (coef_hbm, coef),
        (asc_hbm, asc),
        (availability_hbm, availability),
        (theta_hbm, theta),
        (anchor_district_hbm, anchor_district),
        (district_const_hbm, district_const),
    ]
    loads = [pltpu.make_async_copy(a, b, load_sem.at[i]) for i, (a, b) in enumerate(small)]

    def skim_load(g):
        part = pl.ds(pl.multiple_of(g * GROUP, GROUP), GROUP)
        return pltpu.make_async_copy(skims_hbm.at[:, part], skims.at[:, part], skim_sem.at[g])

    for load in loads:
        load.start()
    for g in range(groups):
        skim_load(g).start()
    for load in loads:
        load.wait()

    seg_hot_t = hot(segment[...] == iota((seg_count, rows), 0))
    worker_hot = seg_hot_t * workers[...]
    eye = hot(iota((rows, rows), 0) == iota((rows, rows), 1))
    seg_col = jnp.sum(eye * segment[...].astype(F32), axis=1, keepdims=True).astype(jnp.int32)
    seg_hot = hot(seg_col == iota((rows, seg_count), 1))
    size_term = jnp.zeros((seg_count, zones), F32)
    for c in range(beta.shape[1]):
        size_term = size_term + beta[:, c : c + 1] * employment[c : c + 1, :].astype(F32)
    sizes[me_dest] = jnp.broadcast_to(jnp.sum(size_term, axis=1, keepdims=True), sizes.shape[1:])
    segs[me_orig] = jnp.broadcast_to(jnp.sum(worker_hot, axis=1, keepdims=True), segs.shape[1:])
    dist_hot[...] = hot(zone_district[...] == iota((dist_count, zones), 0), BF16)

    def by_segment(table):
        out = jnp.zeros((rows, table.shape[1]), F32)
        for s in range(seg_count):
            out = jnp.where(seg_hot[:, s : s + 1] > 0.5, table[s : s + 1, :], out)
        return out

    block = mode_count * GROUP
    width = skim_count * GROUP
    wide = width + 2 * GROUP
    pair = seg_count * mode_count
    column = iota((1, 1, wide), 2)
    pair_eye = hot(iota((pair, pair), 0) == iota((pair, pair), 1))
    widen = hot(iota((skim_count, wide), 1) // GROUP == iota((skim_count, wide), 0), BF16)
    table = dot(dot_nt(pair_eye.astype(BF16), coef[...]).astype(BF16), widen)
    rest = jnp.sum(pair_eye * asc[...], axis=1, keepdims=True)
    for i in range(3):
        part = rest.astype(BF16).astype(F32)
        table = jnp.where(column[0] == width + GROUP + i, part, table)
        rest = rest - part
    table = table.astype(BF16)
    usable = jnp.logical_or(availability[...] > 0, iota((mode_count, rows), 0) == 0)
    closed = jnp.where(usable, 0.0, -1e30)
    keep = jnp.logical_or(
        column % GROUP == iota((1, GROUP, 1), 1), column >= width + GROUP
    )
    for g in range(groups):
        mine = slice(g * GROUP, (g + 1) * GROUP)
        lane_of = seg_col[mine].reshape(1, GROUP, 1) * mode_count + iota((mode_count, 1, 1), 0)
        row_pair = hot(lane_of == iota((1, 1, pair), 2)).reshape(block, pair)
        main = dot(row_pair.astype(BF16), table).reshape(mode_count, GROUP, wide)
        shut = jnp.concatenate(
            [
                jnp.zeros((mode_count, width), F32),
                closed[:, mine],
                jnp.zeros((mode_count, GROUP), F32),
            ],
            axis=1,
        )
        main = jnp.where(keep, main + shut.reshape(mode_count, 1, wide), 0.0)
        weights[g * block : (g + 1) * block, :] = main.reshape(block, wide).astype(BF16)
    ones = jnp.ones((2 * GROUP, TILE), BF16)

    theta_rows[...] = jnp.broadcast_to(
        jnp.sum(seg_hot * theta[...], axis=1, keepdims=True), theta_rows.shape
    )
    anchor_hot_t = hot(anchor_district[...] == iota((dist_count, rows), 0), BF16)
    anchor_hot = dot_nt(eye.astype(BF16), anchor_hot_t)
    anchor_const = dot(anchor_hot, district_const[...], HIGH)
    top, low = halves(anchor_const)
    rest = (anchor_const - top.astype(F32) - low.astype(F32)).astype(BF16)
    pair_const = dot(jnp.concatenate([top, low, rest], axis=0), dist_hot[...])
    pair_const = pair_const[:rows] + (pair_const[rows : 2 * rows] + pair_const[2 * rows :])
    base[...] = by_segment(jnp.log(size_term)) + pair_const

    def group_step(g, carry):
        first = pl.multiple_of(g * GROUP, GROUP)
        skim_load(g).wait()
        mine = pl.ds(pl.multiple_of(g * block, block), block)
        theta_col = theta_rows[pl.ds(first, GROUP), 0:1]
        for t in range(zones // TILE):
            cols = slice(t * TILE, (t + 1) * TILE)
            near = skims[:, pl.ds(first, GROUP), cols].reshape(width, TILE)
            near = jnp.concatenate([near, ones], axis=0)
            utility = dot(weights[mine, :], near).reshape(mode_count, GROUP, TILE)
            peak = jnp.max(utility, axis=0)
            grown = jnp.exp(utility - peak[None])
            total = jnp.sum(grown, axis=0)
            mode_exp[g, :, :, cols] = grown
            inv_total[pl.ds(first, GROUP), cols] = 1.0 / total
            base[pl.ds(first, GROUP), cols] += theta_col * (peak + jnp.log(total))
        return carry

    lax.fori_loop(0, groups, group_step, 0, unroll=True)

    pl.semaphore_wait(barrier, n_dest + n_orig - 2)

    def as_row(col):
        return jnp.sum(eye * col, axis=0, keepdims=True)

    def local_stats(value):
        peak = jnp.max(value, axis=1, keepdims=True)
        grown = jnp.exp(value - peak)
        total = jnp.sum(grown, axis=1, keepdims=True)
        stats[0, me_dest, 0:1, 0:rows] = as_row(peak)
        stats[0, me_dest, 1:2, 0:rows] = as_row(total)
        dest[1].share()
        dest[0].share()
        orig[0].share()
        return grown, peak

    def start_modelled(i, pieces, scale):
        left, left_low = halves(worker_hot * scale)
        both = dot(jnp.concatenate([left, left_low], axis=0), pieces[0])
        parts[i, me_orig] = both[:seg_count] + (dot(left, pieces[1]) + both[seg_count:])
        orig[1 + i].share()

    def end_modelled(i):
        orig[1 + i].landed()
        out = parts[i, 0]
        for j in range(1, n_orig):
            out = out + parts[i, j]
        return out

    grown, local_peak = local_stats(base[...])
    pieces = halves(grown)
    dest[0].landed()
    orig[0].landed()
    size_total, seg_total = sizes[0], segs[0]
    for j in range(1, n_dest):
        size_total = size_total + sizes[j]
    for j in range(1, n_orig):
        seg_total = seg_total + segs[j]
    target = size_term * (seg_total / size_total)[:, 0:1] + 1.0
    dest[1].landed()
    peaks = [stats[0, j, 0:1, 0:rows] for j in range(n_dest)]
    peak = functools.reduce(jnp.maximum, peaks)
    total = jnp.zeros_like(peak)
    for j in range(n_dest):
        total = total + stats[0, j, 1:2, 0:rows] * jnp.exp(peaks[j] - peak)
    start_modelled(0, pieces, jnp.exp(stats[0, me_dest, 0:1, 0:rows] - peak) / total)
    joint_peak = jnp.sum(eye * peak, axis=1, keepdims=True)
    grown = grown * jnp.exp(local_peak - joint_peak)
    base[...] = grown * inv_total[...]
    ratio = target / (end_modelled(0) + 1.0)
    ratio_rows = by_segment(ratio)
    grown = grown * ratio_rows
    base[...] = base[...] * ratio_rows
    stats[1, me_dest, 0:1, 0:rows] = as_row(jnp.sum(grown, axis=1, keepdims=True))
    dest[2].share()

    half = mode_count // 2
    span = half // PIECES
    chunks = groups * PIECES
    size = span * GROUP
    middle = n_dest // 2
    odd = lax.rem(me_orig, 2) == 1
    inward = jnp.where(me_dest < middle, 1, -1)
    inner = jnp.logical_or(me_dest == middle - 1, me_dest == middle)
    outer = jnp.logical_and(me_dest != 0, me_dest != n_dest - 1)
    lane = jnp.where(inner, 1, 0)
    toward = me_dest + inward
    away = jnp.where(outer, me_dest - inward, toward)

    def rows_of(ref, c):
        return ref.at[pl.ds(pl.multiple_of(c * size, size), size)]

    def copy_in(c, slot, place, sem, device, source=flows):
        return pltpu.make_async_remote_copy(
            src_ref=rows_of(source, c),
            dst_ref=rows_of(inbox.at[slot], place),
            send_sem=sum_send.at[0],
            recv_sem=sum_recv.at[sem],
            device_id=device,
            device_id_type=MESH,
        )

    def sum_copy(c, slot, source=flows):
        return copy_in(c, n_dest + slot, c, slot * chunks + c, {"dest": toward}, source)

    def give_copy(c, source):
        sem = source * (chunks // 2) + c // 2
        return copy_in(c, source, c // 2, sem, {"dest": middle - 1 + c % 2})

    def first_copy(c):
        return copy_in(
            c,
            jnp.where(odd, n_dest + lane, me_dest),
            jnp.where(odd, c, c // 2),
            jnp.where(odd, lane * chunks + c, me_dest * (chunks // 2) + c // 2),
            {"dest": jnp.where(odd, toward, middle - 1 + c % 2)},
        )

    def back_copy(c):
        return pltpu.make_async_remote_copy(
            src_ref=rows_of(flow_out, c),
            dst_ref=rows_of(flow_out, c),
            send_sem=back_send.at[0],
            recv_sem=back_recv.at[0],
            device_id={"dest": away},
            device_id_type=MESH,
        )

    def other(i):
        return i + jnp.where(i >= me_dest, 1, 0)

    def turn_copy(k, i):
        c = 2 * k + me_dest - (middle - 1)
        return pltpu.make_async_remote_copy(
            src_ref=rows_of(flow_out, c),
            dst_ref=rows_of(flow_out, c),
            send_sem=turn_send.at[0],
            recv_sem=back_recv.at[0],
            device_id={"dest": other(i)},
            device_id_type=MESH,
        )

    def own_chunk(c):
        g, p = c // PIECES, c % PIECES
        factor = base[g * GROUP : (g + 1) * GROUP, :][None]
        mixed = jnp.concatenate(
            [
                mode_exp[g, k + p * span : k + (p + 1) * span] * factor
                for k in (0, half)
            ],
            axis=0,
        )
        top, low = halves(mixed.reshape(2 * size, zones))
        out = dot_nt(top, dist_hot[...]) + dot_nt(low, dist_hot[...])
        flows[c * size : (c + 1) * size, :] = jnp.concatenate([out[:size], out[size:]], axis=1)

    def joint_total():
        dest[2].landed()
        total = stats[1, 0, 0:1, 0:rows]
        for j in range(1, n_dest):
            total = total + stats[1, j, 0:1, 0:rows]
        start_modelled(1, halves(grown), 1.0 / total)
        access_out[...] = peak + jnp.log(total)
        scale = jnp.sum(eye * (workers[...] / total), axis=1, keepdims=True)
        scale_rows[...] = jnp.broadcast_to(scale, scale_rows.shape)

    def at(c):
        return slice(c * size, (c + 1) * size)

    def gather(c):
        sum_copy(c, 0).wait_recv()
        carry[at(c), :] = flows[at(c), :] + inbox[n_dest, at(c), :]
        sum_copy(c, lane, carry).start()

    def turn(c):
        sum_copy(c, 1).wait_recv()
        flow_out[at(c), :] = carry[at(c), :] + inbox[n_dest + 1, at(c), :]
        back_copy(c).start()

    def ahead_copy(c):
        return pltpu.make_async_remote_copy(
            src_ref=rows_of(ahead, c),
            dst_ref=rows_of(inbox.at[n_dest], c),
            send_sem=back_send.at[0],
            recv_sem=back_recv.at[0],
            device_id={"dest": 0},
            device_id_type=MESH,
        )

    def send_ahead(c):
        sum_copy(c, 1).wait_recv()
        ahead[at(c), :] = flows[at(c), :] + inbox[n_dest + 1, at(c), :]
        ahead_copy(c).start()

    def place_of(k):
        c = 2 * k + me_dest - (middle - 1)
        return pl.ds(pl.multiple_of(c * size, size), size)

    def early_copy(k):
        c = 2 * k + me_dest - (middle - 1)
        return pltpu.make_async_remote_copy(
            src_ref=rows_of(turned, k),
            dst_ref=rows_of(inbox.at[0], c),
            send_sem=turn_send.at[0],
            recv_sem=back_recv.at[0],
            device_id={"dest": 0},
            device_id_type=MESH,
        )

    def serve(k):
        for i in range(1, n_dest - 1):
            give_copy(2 * k, other(i)).wait_recv()
        both = flows[place_of(k), :]
        for i in range(1, n_dest - 1):
            both = both + inbox[other(i), at(k), :]
        turned[at(k), :] = both
        early_copy(k).start()

    def serve_rest(k):
        give_copy(2 * k, 0).wait_recv()
        flow_out[place_of(k), :] = turned[at(k), :] + inbox[0, at(k), :]
        for i in range(1, n_dest - 1):
            turn_copy(k, i).start()

    line_mid = jnp.logical_and(odd, outer)
    serves = jnp.logical_and(jnp.logical_not(odd), inner)
    short = jnp.int32(middle) == 2
    adds = jnp.logical_and(me_dest == 0, jnp.logical_or(jnp.logical_not(odd), short))
    plain = jnp.logical_not(jnp.logical_or(line_mid, serves))

    def not_mine(c):
        return me_dest != middle - 1 + c % 2

    @pl.when(line_mid)
    def _():
        for c in range(chunks):
            own_chunk(c)

    @pl.when(serves)
    def _():
        for c in range(chunks):
            own_chunk(c)
            pl.when(not_mine(c))(lambda c=c: first_copy(c).start())

        for k in range(chunks // 2):
            if k == WAIT:
                joint_total()
            serve(k)
        for k in range(chunks // 2):
            serve_rest(k)

    @pl.when(plain)
    def _():
        for c in range(chunks):
            own_chunk(c)
            first_copy(c).start()

    line_inner = jnp.logical_and(odd, inner)

    leads = jnp.logical_and(line_inner, jnp.logical_and(short, me_dest == 1))

    @pl.when(leads)
    def _():
        for c in range(chunks + LEAD):
            if c == WAIT:
                joint_total()
            if c < chunks:
                gather(c)
            if c >= LEAD:
                send_ahead(c - LEAD)
        flow_out[...] = carry[...] + inbox[n_dest + 1]

    @pl.when(jnp.logical_and(line_inner, jnp.logical_not(leads)))
    def _():
        for c in range(chunks + LAG):
            if c == WAIT:
                joint_total()
            if c < chunks:
                gather(c)
            if c >= LAG:
                turn(c - LAG)

    @pl.when(jnp.logical_not(inner))
    def _():
        joint_total()

        @pl.when(line_mid)
        def _():
            for c in range(chunks):
                gather(c)

    modelled = end_modelled(1)
    modelled_out[...] = modelled
    shadow_out[...] = jnp.log(ratio) + jnp.log(target / (modelled + 1.0))

    def amount(ref, send, recv):
        return pltpu.make_async_remote_copy(
            src_ref=ref,
            dst_ref=ref,
            send_sem=send.at[0],
            recv_sem=recv.at[0],
            device_id={"dest": away},
            device_id_type=MESH,
        )

    @pl.when(jnp.logical_not(jnp.logical_or(line_inner, serves)))
    def _():
        amount(flow_out, back_send, back_recv).wait_recv()

        @pl.when(line_mid)
        def _():
            amount(flow_out, back_send, back_recv).start()

        @pl.when(adds)
        def _():
            flow_out[...] = flows[...] + inbox[jnp.where(odd, n_dest, 0)]

    @pl.when(serves)
    def _():
        amount(turned, sum_send, back_recv).wait_recv()
        amount(turned, sum_send, back_recv).wait_send()
        sent = inbox.at[pl.ds(0, n_dest - 1), pl.ds(0, turned.shape[0])]
        amount(sent, turn_send, back_recv).wait_send()

    @pl.when(jnp.logical_not(serves))
    def _():
        amount(flows, sum_send, back_recv).wait_send()

    @pl.when(line_mid)
    def _():
        amount(flow_out, back_send, back_recv).wait_send()

    for one in dest + orig:
        one.sent()


def finish(
    mode_count, groups, flow, access, modelled, shadow, scale, flow_out, access_out,
    modelled_out, shadow_out, table, spread, sem, table_sem,
):
    copies = [
        pltpu.make_async_copy(a, b, sem.at[i])
        for i, (a, b) in enumerate(
            ((access, access_out), (modelled, modelled_out), (shadow, shadow_out))
        )
    ]
    for copy in copies:
        copy.start()
    lanes = flow.shape[1]
    half = mode_count // 2
    rows = groups * GROUP
    width = table.shape[1]
    source = iota((2 * lanes, 1), 0)
    place = source % (lanes // 2) * mode_count + source // lanes
    place = place + source % lanes // (lanes // 2) * half
    starts = [(t, m) for t in range(0, width, TILE) for m in range(0, half, 2)]
    for i, (t, m) in enumerate(starts):
        spread[i] = hot(iota((2 * lanes, TILE), 1) == place + (m - t), BF16)
    pieces = flow[...].reshape(groups, half, GROUP, lanes)
    pieces = pieces * scale[...].reshape(groups, 1, GROUP, lanes)
    pairs = []
    for m in range(0, half, 2):
        pair = [pieces[:, m + i].reshape(rows, lanes) for i in range(2)]
        pairs.append(jnp.concatenate(halves(jnp.concatenate(pair, axis=1)), axis=0))
    for t in range(0, width, TILE):
        total = jnp.zeros((2 * rows, TILE), F32)
        for i, (start, m) in enumerate(starts):
            if start == t:
                total = total + dot(pairs[m // 2], spread[i])
        cols = slice(t, t + TILE)
        table[:, cols] = total[:rows] + total[rows:]
        copy = pltpu.make_async_copy(
            table.at[:, cols], flow_out.at[:, cols], table_sem.at[t // TILE]
        )
        copy.start()
        copies.append(copy)
    for copy in copies:
        copy.wait()


def per_device(
    n_dest,
    n_orig,
    skims,
    coef,
    asc,
    theta,
    beta,
    employment,
    zone_district,
    anchor_district,
    district_const,
    segment,
    availability,
    workers,
):
    skim_count, rows, zones = skims.shape
    seg_count = theta.shape[0]
    mode_count = availability.shape[1]
    dist_count = district_const.shape[0]
    groups = rows // GROUP
    inputs = (
        skims,
        coef.T,
        asc.reshape(1, -1),
        theta.reshape(1, -1),
        beta,
        employment,
        zone_district.reshape(1, -1),
        anchor_district.reshape(1, -1),
        district_const,
        segment.reshape(1, -1),
        availability.T,
        workers.reshape(1, -1),
    )
    flow_rows = rows * mode_count // 2
    lanes = max(128, rows)
    chunks = groups * PIECES
    vmem = pl.BlockSpec(memory_space=pltpu.VMEM)
    sem = pltpu.SemaphoreType.DMA
    access, flow, modelled, shadow, scale = pl.pallas_call(
        functools.partial(kernel, n_dest, n_orig),
        out_shape=(
            pltpu.VMEM((1, rows), F32),
            pltpu.VMEM((flow_rows, 2 * dist_count), F32),
            pltpu.VMEM((seg_count, zones), F32),
            pltpu.VMEM((seg_count, zones), F32),
            pltpu.VMEM((rows, 2 * dist_count), F32),
        ),
        in_specs=[pl.BlockSpec(memory_space=pl.ANY)] * 12,
        out_specs=(vmem,) * 5,
        scratch_shapes=[pltpu.VMEM(x.shape, x.dtype) for x in inputs]
        + [
            pltpu.VMEM((groups, mode_count, GROUP, zones), F32),
            pltpu.VMEM((rows, zones), F32),
            pltpu.VMEM((rows * mode_count, (skims.shape[0] + 2) * GROUP), BF16),
            pltpu.VMEM((rows, 128), F32),
            pltpu.VMEM((rows, zones), F32),
            pltpu.VMEM((dist_count, zones), BF16),
            pltpu.VMEM((n_dest, seg_count, 128), F32),
            pltpu.VMEM((n_orig, seg_count, 128), F32),
            pltpu.VMEM((2, n_dest, 8, lanes), F32),
            pltpu.VMEM((2, n_orig, seg_count, zones), F32),
            pltpu.VMEM((flow_rows, 2 * dist_count), F32),
            pltpu.VMEM((n_dest + 2, flow_rows, 2 * dist_count), F32),
            pltpu.VMEM((flow_rows // 2, 2 * dist_count), F32),
            pltpu.VMEM((flow_rows, 2 * dist_count), F32),
            pltpu.VMEM((flow_rows, 2 * dist_count), F32),
            sem((3,)),
            sem((3,)),
            sem((3,)),
            sem((3,)),
            sem((1,)),
            sem((max(n_dest * (chunks // 2), 2 * chunks),)),
            sem((1,)),
            sem((1,)),
            sem((1,)),
            sem((groups,)),
            sem((len(inputs) - 1,)),
        ],
        compiler_params=pltpu.CompilerParams(
            collective_id=0, has_side_effects=True, vmem_limit_bytes=33554432
        ),
    )(*(pltpu.with_memory_space_constraint(x, pltpu.HBM) for x in inputs))
    anywhere = pl.BlockSpec(memory_space=pl.ANY)
    width = dist_count * mode_count
    results = [
        pltpu.with_memory_space_constraint(x, pltpu.VMEM)
        for x in (flow, access, modelled, shadow, scale)
    ]
    flow, access, modelled, shadow = pl.pallas_call(
        functools.partial(finish, mode_count, groups),
        out_shape=(jax.ShapeDtypeStruct((rows, dist_count * mode_count), F32),)
        + tuple(jax.ShapeDtypeStruct(x.shape, x.dtype) for x in results[1:4]),
        in_specs=[vmem] * 5,
        out_specs=(anywhere,) * 4,
        scratch_shapes=[
            pltpu.VMEM((rows, width), F32),
            pltpu.VMEM((width // TILE * (mode_count // 4), 4 * dist_count, TILE), BF16),
            sem((3,)),
            sem((width // TILE,)),
        ],
        compiler_params=pltpu.CompilerParams(vmem_limit_bytes=16777216),
    )(*results)
    return access.reshape(rows), flow, modelled, shadow


def solution(mesh):
    return jax.shard_map(
        functools.partial(per_device, mesh.shape["dest"], mesh.shape["orig"]),
        mesh=mesh,
        in_specs=(
            P(None, ("scen", "orig"), "dest"),
            P(),
            P(),
            P(),
            P(),
            P(None, ("scen", "dest")),
            P("dest"),
            P(("scen", "orig")),
            P(),
            P(("scen", "orig")),
            P(("scen", "orig"), None),
            P(("scen", "orig")),
        ),
        out_specs=(
            P(("scen", "orig")),
            P(("scen", "orig"), None),
            P(None, ("scen", "dest")),
            P(None, ("scen", "dest")),
        ),
        check_vma=False,
    )
```

```python
import functools

import jax
import jax.numpy as jnp
from jax import lax
from jax.experimental import pallas as pl
from jax.experimental.pallas import tpu as pltpu
from jax.sharding import PartitionSpec as P

HIGH = lax.Precision.HIGHEST
F32 = jnp.float32
BF16 = jnp.bfloat16
MESH = pl.DeviceIdType.MESH
GROUP = 16
TILE = 256
PIECES = 2
LAG = 4
LEAD = 2
WAIT = 2


def iota(shape, dim):
    return lax.broadcasted_iota(jnp.int32, shape, dim)


def hot(mask, dtype=F32):
    return jnp.where(mask, 1.0, 0.0).astype(dtype)


def dot(a, b, precision=None):
    return jnp.dot(a, b, preferred_element_type=F32, precision=precision)


def dot_nt(a, b):
    return lax.dot_general(a, b, (((1,), (1,)), ((), ())), preferred_element_type=F32)


def halves(x):
    top = x.astype(BF16)
    return top, (x - top.astype(F32)).astype(BF16)


class Exchange:
    def __init__(self, axis, count, send_sem, recv_sem, buf):
        self.axis, self.count, self.buf = axis, count, buf
        self.send_sem, self.recv_sem = send_sem, recv_sem

    def copy(self, part, k):
        me = lax.axis_index(self.axis)
        return pltpu.make_async_remote_copy(
            src_ref=self.buf.at[part],
            dst_ref=self.buf.at[part],
            send_sem=self.send_sem,
            recv_sem=self.recv_sem,
            device_id={self.axis: lax.rem(me + k, self.count)},
            device_id_type=MESH,
        )

    def share(self):
        for k in range(1, self.count):
            self.copy(lax.axis_index(self.axis), k).start()

    def landed(self):
        self.copy(pl.ds(0, self.count - 1), 1).wait_recv()

    def sent(self):
        self.copy(pl.ds(0, self.count - 1), 1).wait_send()


def kernel(
    n_dest,
    n_orig,
    skims_hbm,
    coef_hbm,
    asc_hbm,
    theta_hbm,
    beta_hbm,
    employment_hbm,
    zone_district_hbm,
    anchor_district_hbm,
    district_const_hbm,
    segment_hbm,
    availability_hbm,
    workers_hbm,
    access_out,
    flow_out,
    modelled_out,
    shadow_out,
    scale_rows,
    spread,
    skims,
    coef,
    asc,
    theta,
    beta,
    employment,
    zone_district,
    anchor_district,
    district_const,
    segment,
    availability,
    workers,
    mode_exp,
    inv_total,
    weights,
    theta_rows,
    base,
    dist_hot,
    sizes,
    segs,
    stats,
    parts,
    flows,
    inbox,
    turned,
    carry,
    ahead,
    dest_send,
    dest_recv,
    orig_send,
    orig_recv,
    sum_send,
    sum_recv,
    back_send,
    back_recv,
    turn_send,
    skim_sem,
    load_sem,
):
    skim_count, rows, zones = skims.shape
    seg_count = theta.shape[1]
    mode_count = availability.shape[0]
    dist_count = district_const.shape[0]
    groups = rows // GROUP
    me_dest = lax.axis_index("dest")
    me_orig = lax.axis_index("orig")
    dest = [
        Exchange("dest", n_dest, dest_send.at[i], dest_recv.at[i], buf)
        for i, buf in enumerate((sizes, stats.at[0], stats.at[1]))
    ]
    orig = [
        Exchange("orig", n_orig, orig_send.at[i], orig_recv.at[i], buf)
        for i, buf in enumerate((segs, parts.at[0], parts.at[1]))
    ]

    barrier = pltpu.get_barrier_semaphore()
    for axis, me, count in (("dest", me_dest, n_dest), ("orig", me_orig, n_orig)):
        for k in range(1, count):
            pl.semaphore_signal(
                barrier,
                inc=1,
                device_id={axis: lax.rem(me + k, count)},
                device_id_type=MESH,
            )
    small = [
        (segment_hbm, segment),
        (workers_hbm, workers),
        (beta_hbm, beta),
        (employment_hbm, employment),
        (zone_district_hbm, zone_district),
        (coef_hbm, coef),
        (asc_hbm, asc),
        (availability_hbm, availability),
        (theta_hbm, theta),
        (anchor_district_hbm, anchor_district),
        (district_const_hbm, district_const),
    ]
    loads = [pltpu.make_async_copy(a, b, load_sem.at[i]) for i, (a, b) in enumerate(small)]

    def skim_load(g):
        part = pl.ds(pl.multiple_of(g * GROUP, GROUP), GROUP)
        return pltpu.make_async_copy(skims_hbm.at[:, part], skims.at[:, part], skim_sem.at[g])

    for load in loads:
        load.start()
    for g in range(groups):
        skim_load(g).start()
    for load in loads:
        load.wait()

    seg_hot_t = hot(segment[...] == iota((seg_count, rows), 0))
    worker_hot = seg_hot_t * workers[...]
    eye = hot(iota((rows, rows), 0) == iota((rows, rows), 1))
    seg_col = jnp.sum(eye * segment[...].astype(F32), axis=1, keepdims=True).astype(jnp.int32)
    seg_hot = hot(seg_col == iota((rows, seg_count), 1))
    size_term = jnp.zeros((seg_count, zones), F32)
    for c in range(beta.shape[1]):
        size_term = size_term + beta[:, c : c + 1] * employment[c : c + 1, :].astype(F32)
    sizes[me_dest] = jnp.broadcast_to(jnp.sum(size_term, axis=1, keepdims=True), sizes.shape[1:])
    segs[me_orig] = jnp.broadcast_to(jnp.sum(worker_hot, axis=1, keepdims=True), segs.shape[1:])
    dist_hot[...] = hot(zone_district[...] == iota((dist_count, zones), 0), BF16)

    def by_segment(table):
        out = jnp.zeros((rows, table.shape[1]), F32)
        for s in range(seg_count):
            out = jnp.where(seg_hot[:, s : s + 1] > 0.5, table[s : s + 1, :], out)
        return out

    block = mode_count * GROUP
    width = skim_count * GROUP
    wide = width + 2 * GROUP
    pair = seg_count * mode_count
    column = iota((1, 1, wide), 2)
    pair_eye = hot(iota((pair, pair), 0) == iota((pair, pair), 1))
    widen = hot(iota((skim_count, wide), 1) // GROUP == iota((skim_count, wide), 0), BF16)
    table = dot(dot_nt(pair_eye.astype(BF16), coef[...]).astype(BF16), widen)
    rest = jnp.sum(pair_eye * asc[...], axis=1, keepdims=True)
    for i in range(3):
        part = rest.astype(BF16).astype(F32)
        table = jnp.where(column[0] == width + GROUP + i, part, table)
        rest = rest - part
    table = table.astype(BF16)
    usable = jnp.logical_or(availability[...] > 0, iota((mode_count, rows), 0) == 0)
    closed = jnp.where(usable, 0.0, -1e30)
    keep = jnp.logical_or(
        column % GROUP == iota((1, GROUP, 1), 1), column >= width + GROUP
    )
    for g in range(groups):
        mine = slice(g * GROUP, (g + 1) * GROUP)
        lane_of = seg_col[mine].reshape(1, GROUP, 1) * mode_count + iota((mode_count, 1, 1), 0)
        row_pair = hot(lane_of == iota((1, 1, pair), 2)).reshape(block, pair)
        main = dot(row_pair.astype(BF16), table).reshape(mode_count, GROUP, wide)
        shut = jnp.concatenate(
            [
                jnp.zeros((mode_count, width), F32),
                closed[:, mine],
                jnp.zeros((mode_count, GROUP), F32),
            ],
            axis=1,
        )
        main = jnp.where(keep, main + shut.reshape(mode_count, 1, wide), 0.0)
        weights[g * block : (g + 1) * block, :] = main.reshape(block, wide).astype(BF16)
    ones = jnp.ones((2 * GROUP, TILE), BF16)

    theta_rows[...] = jnp.broadcast_to(
        jnp.sum(seg_hot * theta[...], axis=1, keepdims=True), theta_rows.shape
    )
    anchor_hot_t = hot(anchor_district[...] == iota((dist_count, rows), 0), BF16)
    anchor_hot = dot_nt(eye.astype(BF16), anchor_hot_t)
    anchor_const = dot(anchor_hot, district_const[...], HIGH)
    top, low = halves(anchor_const)
    rest = (anchor_const - top.astype(F32) - low.astype(F32)).astype(BF16)
    pair_const = dot(jnp.concatenate([top, low, rest], axis=0), dist_hot[...])
    pair_const = pair_const[:rows] + (pair_const[rows : 2 * rows] + pair_const[2 * rows :])
    base[...] = by_segment(jnp.log(size_term)) + pair_const

    def group_step(g, carry):
        first = pl.multiple_of(g * GROUP, GROUP)
        skim_load(g).wait()
        mine = pl.ds(pl.multiple_of(g * block, block), block)
        theta_col = theta_rows[pl.ds(first, GROUP), 0:1]
        for t in range(zones // TILE):
            cols = slice(t * TILE, (t + 1) * TILE)
            near = skims[:, pl.ds(first, GROUP), cols].reshape(width, TILE)
            near = jnp.concatenate([near, ones], axis=0)
            utility = dot(weights[mine, :], near).reshape(mode_count, GROUP, TILE)
            peak = jnp.max(utility, axis=0)
            grown = jnp.exp(utility - peak[None])
            total = jnp.sum(grown, axis=0)
            mode_exp[g, :, :, cols] = grown
            inv_total[pl.ds(first, GROUP), cols] = 1.0 / total
            base[pl.ds(first, GROUP), cols] += theta_col * (peak + jnp.log(total))
        return carry

    lax.fori_loop(0, groups, group_step, 0, unroll=True)

    pl.semaphore_wait(barrier, n_dest + n_orig - 2)

    def as_row(col):
        return jnp.sum(eye * col, axis=0, keepdims=True)

    def local_stats(value):
        peak = jnp.max(value, axis=1, keepdims=True)
        grown = jnp.exp(value - peak)
        total = jnp.sum(grown, axis=1, keepdims=True)
        stats[0, me_dest, 0:1, 0:rows] = as_row(peak)
        stats[0, me_dest, 1:2, 0:rows] = as_row(total)
        dest[1].share()
        dest[0].share()
        orig[0].share()
        return grown, peak

    def start_modelled(i, pieces, scale):
        left, left_low = halves(worker_hot * scale)
        both = dot(jnp.concatenate([left, left_low], axis=0), pieces[0])
        parts[i, me_orig] = both[:seg_count] + (dot(left, pieces[1]) + both[seg_count:])
        orig[1 + i].share()

    def end_modelled(i):
        orig[1 + i].landed()
        out = parts[i, 0]
        for j in range(1, n_orig):
            out = out + parts[i, j]
        return out

    grown, local_peak = local_stats(base[...])
    pieces = halves(grown)
    dest[0].landed()
    orig[0].landed()
    size_total, seg_total = sizes[0], segs[0]
    for j in range(1, n_dest):
        size_total = size_total + sizes[j]
    for j in range(1, n_orig):
        seg_total = seg_total + segs[j]
    target = size_term * (seg_total / size_total)[:, 0:1] + 1.0
    dest[1].landed()
    peaks = [stats[0, j, 0:1, 0:rows] for j in range(n_dest)]
    peak = functools.reduce(jnp.maximum, peaks)
    total = jnp.zeros_like(peak)
    for j in range(n_dest):
        total = total + stats[0, j, 1:2, 0:rows] * jnp.exp(peaks[j] - peak)
    start_modelled(0, pieces, jnp.exp(stats[0, me_dest, 0:1, 0:rows] - peak) / total)
    joint_peak = jnp.sum(eye * peak, axis=1, keepdims=True)
    grown = grown * jnp.exp(local_peak - joint_peak)
    base[...] = grown * inv_total[...]
    lanes = 2 * dist_count
    half = mode_count // 2
    width_out = dist_count * mode_count
    source = iota((2 * lanes, 1), 0)
    place = source % dist_count * mode_count + source // lanes
    place = place + source % lanes // dist_count * half
    starts = [(t, m) for t in range(0, width_out, TILE) for m in range(0, half, 2)]
    for i, (t, m) in enumerate(starts):
        spread[i] = hot(iota((2 * lanes, TILE), 1) == place + (m - t), BF16)
    ratio = target / (end_modelled(0) + 1.0)
    ratio_rows = by_segment(ratio)
    grown = grown * ratio_rows
    base[...] = base[...] * ratio_rows
    stats[1, me_dest, 0:1, 0:rows] = as_row(jnp.sum(grown, axis=1, keepdims=True))
    dest[2].share()

    half = mode_count // 2
    span = half // PIECES
    chunks = groups * PIECES
    size = span * GROUP
    middle = n_dest // 2
    odd = lax.rem(me_orig, 2) == 1
    inward = jnp.where(me_dest < middle, 1, -1)
    inner = jnp.logical_or(me_dest == middle - 1, me_dest == middle)
    outer = jnp.logical_and(me_dest != 0, me_dest != n_dest - 1)
    lane = jnp.where(inner, 1, 0)
    toward = me_dest + inward
    away = jnp.where(outer, me_dest - inward, toward)

    def rows_of(ref, c):
        return ref.at[pl.ds(pl.multiple_of(c * size, size), size)]

    def copy_in(c, slot, place, sem, device, source=flows):
        return pltpu.make_async_remote_copy(
            src_ref=rows_of(source, c),
            dst_ref=rows_of(inbox.at[slot], place),
            send_sem=sum_send.at[0],
            recv_sem=sum_recv.at[sem],
            device_id=device,
            device_id_type=MESH,
        )

    def sum_copy(c, slot, source=flows):
        return copy_in(c, n_dest + slot, c, slot * chunks + c, {"dest": toward}, source)

    def give_copy(c, source):
        sem = source * (chunks // 2) + c // 2
        return copy_in(c, source, c // 2, sem, {"dest": middle - 1 + c % 2})

    def first_copy(c):
        return copy_in(
            c,
            jnp.where(odd, n_dest + lane, me_dest),
            jnp.where(odd, c, c // 2),
            jnp.where(odd, lane * chunks + c, me_dest * (chunks // 2) + c // 2),
            {"dest": jnp.where(odd, toward, middle - 1 + c % 2)},
        )

    def back_copy(c):
        return pltpu.make_async_remote_copy(
            src_ref=rows_of(flow_out, c),
            dst_ref=rows_of(flow_out, c),
            send_sem=back_send.at[0],
            recv_sem=back_recv.at[0],
            device_id={"dest": away},
            device_id_type=MESH,
        )

    def other(i):
        return i + jnp.where(i >= me_dest, 1, 0)

    def turn_copy(k, i):
        c = 2 * k + me_dest - (middle - 1)
        return pltpu.make_async_remote_copy(
            src_ref=rows_of(flow_out, c),
            dst_ref=rows_of(flow_out, c),
            send_sem=turn_send.at[0],
            recv_sem=back_recv.at[0],
            device_id={"dest": other(i)},
            device_id_type=MESH,
        )

    def own_chunk(c):
        g, p = c // PIECES, c % PIECES
        factor = base[g * GROUP : (g + 1) * GROUP, :][None]
        mixed = jnp.concatenate(
            [
                mode_exp[g, k + p * span : k + (p + 1) * span] * factor
                for k in (0, half)
            ],
            axis=0,
        )
        top, low = halves(mixed.reshape(2 * size, zones))
        out = dot_nt(top, dist_hot[...]) + dot_nt(low, dist_hot[...])
        flows[c * size : (c + 1) * size, :] = jnp.concatenate([out[:size], out[size:]], axis=1)

    def joint_total():
        dest[2].landed()
        total = stats[1, 0, 0:1, 0:rows]
        for j in range(1, n_dest):
            total = total + stats[1, j, 0:1, 0:rows]
        start_modelled(1, halves(grown), 1.0 / total)
        access_out[...] = peak + jnp.log(total)
        scale = jnp.sum(eye * (workers[...] / total), axis=1, keepdims=True)
        scale_rows[...] = jnp.broadcast_to(scale, scale_rows.shape)

    def at(c):
        return slice(c * size, (c + 1) * size)

    def gather(c):
        sum_copy(c, 0).wait_recv()
        carry[at(c), :] = flows[at(c), :] + inbox[n_dest, at(c), :]
        sum_copy(c, lane, carry).start()

    def turn(c):
        sum_copy(c, 1).wait_recv()
        flow_out[at(c), :] = carry[at(c), :] + inbox[n_dest + 1, at(c), :]
        back_copy(c).start()

    def ahead_copy(c):
        return pltpu.make_async_remote_copy(
            src_ref=rows_of(ahead, c),
            dst_ref=rows_of(inbox.at[n_dest], c),
            send_sem=back_send.at[0],
            recv_sem=back_recv.at[0],
            device_id={"dest": 0},
            device_id_type=MESH,
        )

    def send_ahead(c):
        sum_copy(c, 1).wait_recv()
        ahead[at(c), :] = flows[at(c), :] + inbox[n_dest + 1, at(c), :]
        ahead_copy(c).start()

    def place_of(k):
        c = 2 * k + me_dest - (middle - 1)
        return pl.ds(pl.multiple_of(c * size, size), size)

    def early_copy(k):
        c = 2 * k + me_dest - (middle - 1)
        return pltpu.make_async_remote_copy(
            src_ref=rows_of(turned, k),
            dst_ref=rows_of(inbox.at[0], c),
            send_sem=turn_send.at[0],
            recv_sem=back_recv.at[0],
            device_id={"dest": 0},
            device_id_type=MESH,
        )

    def serve(k):
        for i in range(1, n_dest - 1):
            give_copy(2 * k, other(i)).wait_recv()
        both = flows[place_of(k), :]
        for i in range(1, n_dest - 1):
            both = both + inbox[other(i), at(k), :]
        turned[at(k), :] = both
        early_copy(k).start()

    def serve_rest(k):
        give_copy(2 * k, 0).wait_recv()
        flow_out[place_of(k), :] = turned[at(k), :] + inbox[0, at(k), :]
        for i in range(1, n_dest - 1):
            turn_copy(k, i).start()

    line_mid = jnp.logical_and(odd, outer)
    serves = jnp.logical_and(jnp.logical_not(odd), inner)
    short = jnp.int32(middle) == 2
    adds = jnp.logical_and(me_dest == 0, jnp.logical_or(jnp.logical_not(odd), short))
    plain = jnp.logical_not(jnp.logical_or(line_mid, serves))

    def not_mine(c):
        return me_dest != middle - 1 + c % 2

    @pl.when(line_mid)
    def _():
        for c in range(chunks):
            own_chunk(c)

    @pl.when(serves)
    def _():
        for c in range(chunks):
            own_chunk(c)
            pl.when(not_mine(c))(lambda c=c: first_copy(c).start())

        for k in range(chunks // 2):
            if k == WAIT:
                joint_total()
            serve(k)
        for k in range(chunks // 2):
            serve_rest(k)

    @pl.when(plain)
    def _():
        for c in range(chunks):
            own_chunk(c)
            first_copy(c).start()

    line_inner = jnp.logical_and(odd, inner)

    leads = jnp.logical_and(line_inner, jnp.logical_and(short, me_dest == 1))

    @pl.when(leads)
    def _():
        for c in range(chunks + LEAD):
            if c == WAIT:
                joint_total()
            if c < chunks:
                gather(c)
            if c >= LEAD:
                send_ahead(c - LEAD)
        flow_out[...] = carry[...] + inbox[n_dest + 1]

    @pl.when(jnp.logical_and(line_inner, jnp.logical_not(leads)))
    def _():
        for c in range(chunks + LAG):
            if c == WAIT:
                joint_total()
            if c < chunks:
                gather(c)
            if c >= LAG:
                turn(c - LAG)

    @pl.when(jnp.logical_not(inner))
    def _():
        joint_total()

        @pl.when(line_mid)
        def _():
            for c in range(chunks):
                gather(c)

    modelled = end_modelled(1)
    modelled_out[...] = modelled
    shadow_out[...] = jnp.log(ratio) + jnp.log(target / (modelled + 1.0))

    def amount(ref, send, recv):
        return pltpu.make_async_remote_copy(
            src_ref=ref,
            dst_ref=ref,
            send_sem=send.at[0],
            recv_sem=recv.at[0],
            device_id={"dest": away},
            device_id_type=MESH,
        )

    @pl.when(jnp.logical_not(jnp.logical_or(line_inner, serves)))
    def _():
        amount(flow_out, back_send, back_recv).wait_recv()

        @pl.when(line_mid)
        def _():
            amount(flow_out, back_send, back_recv).start()

        @pl.when(adds)
        def _():
            flow_out[...] = flows[...] + inbox[jnp.where(odd, n_dest, 0)]

    @pl.when(serves)
    def _():
        amount(turned, sum_send, back_recv).wait_recv()
        amount(turned, sum_send, back_recv).wait_send()
        sent = inbox.at[pl.ds(0, n_dest - 1), pl.ds(0, turned.shape[0])]
        amount(sent, turn_send, back_recv).wait_send()

    @pl.when(jnp.logical_not(serves))
    def _():
        amount(flows, sum_send, back_recv).wait_send()

    @pl.when(line_mid)
    def _():
        amount(flow_out, back_send, back_recv).wait_send()

    for one in dest + orig:
        one.sent()


def finish(
    mode_count, groups, flow, access, modelled, shadow, scale, spread, flow_out, access_out,
    modelled_out, shadow_out, table, sem, table_sem,
):
    copies = [
        pltpu.make_async_copy(a, b, sem.at[i])
        for i, (a, b) in enumerate(
            ((access, access_out), (modelled, modelled_out), (shadow, shadow_out))
        )
    ]
    for copy in copies:
        copy.start()
    lanes = flow.shape[1]
    half = mode_count // 2
    rows = groups * GROUP
    width = table.shape[1]
    starts = [(t, m) for t in range(0, width, TILE) for m in range(0, half, 2)]
    pieces = flow[...].reshape(groups, half, GROUP, lanes)
    pieces = pieces * scale[...].reshape(groups, 1, GROUP, lanes)
    pairs = []
    for m in range(0, half, 2):
        pair = [pieces[:, m + i].reshape(rows, lanes) for i in range(2)]
        pairs.append(jnp.concatenate(halves(jnp.concatenate(pair, axis=1)), axis=0))
    for t in range(0, width, TILE):
        total = jnp.zeros((2 * rows, TILE), F32)
        for i, (start, m) in enumerate(starts):
            if start == t:
                total = total + dot(pairs[m // 2], spread[i])
        cols = slice(t, t + TILE)
        table[:, cols] = total[:rows] + total[rows:]
        copy = pltpu.make_async_copy(
            table.at[:, cols], flow_out.at[:, cols], table_sem.at[t // TILE]
        )
        copy.start()
        copies.append(copy)
    for copy in copies:
        copy.wait()


def per_device(
    n_dest,
    n_orig,
    skims,
    coef,
    asc,
    theta,
    beta,
    employment,
    zone_district,
    anchor_district,
    district_const,
    segment,
    availability,
    workers,
):
    skim_count, rows, zones = skims.shape
    seg_count = theta.shape[0]
    mode_count = availability.shape[1]
    dist_count = district_const.shape[0]
    groups = rows // GROUP
    inputs = (
        skims,
        coef.T,
        asc.reshape(1, -1),
        theta.reshape(1, -1),
        beta,
        employment,
        zone_district.reshape(1, -1),
        anchor_district.reshape(1, -1),
        district_const,
        segment.reshape(1, -1),
        availability.T,
        workers.reshape(1, -1),
    )
    flow_rows = rows * mode_count // 2
    lanes = max(128, rows)
    chunks = groups * PIECES
    width = dist_count * mode_count
    vmem = pl.BlockSpec(memory_space=pltpu.VMEM)
    sem = pltpu.SemaphoreType.DMA
    access, flow, modelled, shadow, scale, spread = pl.pallas_call(
        functools.partial(kernel, n_dest, n_orig),
        out_shape=(
            pltpu.VMEM((1, rows), F32),
            pltpu.VMEM((flow_rows, 2 * dist_count), F32),
            pltpu.VMEM((seg_count, zones), F32),
            pltpu.VMEM((seg_count, zones), F32),
            pltpu.VMEM((rows, 2 * dist_count), F32),
            pltpu.VMEM((width // TILE * (mode_count // 4), 4 * dist_count, TILE), BF16),
        ),
        in_specs=[pl.BlockSpec(memory_space=pl.ANY)] * 12,
        out_specs=(vmem,) * 6,
        scratch_shapes=[pltpu.VMEM(x.shape, x.dtype) for x in inputs]
        + [
            pltpu.VMEM((groups, mode_count, GROUP, zones), F32),
            pltpu.VMEM((rows, zones), F32),
            pltpu.VMEM((rows * mode_count, (skims.shape[0] + 2) * GROUP), BF16),
            pltpu.VMEM((rows, 128), F32),
            pltpu.VMEM((rows, zones), F32),
            pltpu.VMEM((dist_count, zones), BF16),
            pltpu.VMEM((n_dest, seg_count, 128), F32),
            pltpu.VMEM((n_orig, seg_count, 128), F32),
            pltpu.VMEM((2, n_dest, 8, lanes), F32),
            pltpu.VMEM((2, n_orig, seg_count, zones), F32),
            pltpu.VMEM((flow_rows, 2 * dist_count), F32),
            pltpu.VMEM((n_dest + 2, flow_rows, 2 * dist_count), F32),
            pltpu.VMEM((flow_rows // 2, 2 * dist_count), F32),
            pltpu.VMEM((flow_rows, 2 * dist_count), F32),
            pltpu.VMEM((flow_rows, 2 * dist_count), F32),
            sem((3,)),
            sem((3,)),
            sem((3,)),
            sem((3,)),
            sem((1,)),
            sem((max(n_dest * (chunks // 2), 2 * chunks),)),
            sem((1,)),
            sem((1,)),
            sem((1,)),
            sem((groups,)),
            sem((len(inputs) - 1,)),
        ],
        compiler_params=pltpu.CompilerParams(
            collective_id=0, has_side_effects=True, vmem_limit_bytes=33554432
        ),
    )(*(pltpu.with_memory_space_constraint(x, pltpu.HBM) for x in inputs))
    anywhere = pl.BlockSpec(memory_space=pl.ANY)
    results = [
        pltpu.with_memory_space_constraint(x, pltpu.VMEM)
        for x in (flow, access, modelled, shadow, scale, spread)
    ]
    flow, access, modelled, shadow = pl.pallas_call(
        functools.partial(finish, mode_count, groups),
        out_shape=(jax.ShapeDtypeStruct((rows, dist_count * mode_count), F32),)
        + tuple(jax.ShapeDtypeStruct(x.shape, x.dtype) for x in results[1:4]),
        in_specs=[vmem] * 6,
        out_specs=(anywhere,) * 4,
        scratch_shapes=[
            pltpu.VMEM((rows, width), F32),
            sem((3,)),
            sem((width // TILE,)),
        ],
        compiler_params=pltpu.CompilerParams(vmem_limit_bytes=16777216),
    )(*results)
    return access.reshape(rows), flow, modelled, shadow


def solution(mesh):
    return jax.shard_map(
        functools.partial(per_device, mesh.shape["dest"], mesh.shape["orig"]),
        mesh=mesh,
        in_specs=(
            P(None, ("scen", "orig"), "dest"),
            P(),
            P(),
            P(),
            P(),
            P(None, ("scen", "dest")),
            P("dest"),
            P(("scen", "orig")),
            P(),
            P(("scen", "orig")),
            P(("scen", "orig"), None),
            P(("scen", "orig")),
        ),
        out_specs=(
            P(("scen", "orig")),
            P(("scen", "orig"), None),
            P(None, ("scen", "dest")),
            P(None, ("scen", "dest")),
        ),
        check_vma=False,
    )
```

```python
import functools

import jax
import jax.numpy as jnp
from jax import lax
from jax.experimental import pallas as pl
from jax.experimental.pallas import tpu as pltpu
from jax.sharding import PartitionSpec as P

HIGH = lax.Precision.HIGHEST
F32 = jnp.float32
BF16 = jnp.bfloat16
MESH = pl.DeviceIdType.MESH
GROUP = 16
TILE = 256
PIECES = 2
LAG = 4
LEAD = 2
WAIT = 2


def iota(shape, dim):
    return lax.broadcasted_iota(jnp.int32, shape, dim)


def hot(mask, dtype=F32):
    return jnp.where(mask, 1.0, 0.0).astype(dtype)


def dot(a, b, precision=None):
    return jnp.dot(a, b, preferred_element_type=F32, precision=precision)


def dot_nt(a, b):
    return lax.dot_general(a, b, (((1,), (1,)), ((), ())), preferred_element_type=F32)


def halves(x):
    top = x.astype(BF16)
    return top, (x - top.astype(F32)).astype(BF16)


class Exchange:
    def __init__(self, axis, count, send_sem, recv_sem, buf):
        self.axis, self.count, self.buf = axis, count, buf
        self.send_sem, self.recv_sem = send_sem, recv_sem

    def copy(self, part, k):
        me = lax.axis_index(self.axis)
        return pltpu.make_async_remote_copy(
            src_ref=self.buf.at[part],
            dst_ref=self.buf.at[part],
            send_sem=self.send_sem,
            recv_sem=self.recv_sem,
            device_id={self.axis: lax.rem(me + k, self.count)},
            device_id_type=MESH,
        )

    def share(self):
        for k in sorted(range(1, self.count), key=lambda k: abs(2 * k - self.count)):
            self.copy(lax.axis_index(self.axis), k).start()

    def landed(self):
        self.copy(pl.ds(0, self.count - 1), 1).wait_recv()

    def sent(self):
        self.copy(pl.ds(0, self.count - 1), 1).wait_send()


def kernel(
    n_dest,
    n_orig,
    skims_hbm,
    coef_hbm,
    asc_hbm,
    theta_hbm,
    beta_hbm,
    employment_hbm,
    zone_district_hbm,
    anchor_district_hbm,
    district_const_hbm,
    segment_hbm,
    availability_hbm,
    workers_hbm,
    access_out,
    flow_out,
    modelled_out,
    shadow_out,
    scale_rows,
    spread,
    skims,
    coef,
    asc,
    theta,
    beta,
    employment,
    zone_district,
    anchor_district,
    district_const,
    segment,
    availability,
    workers,
    mode_exp,
    inv_total,
    weights,
    theta_rows,
    base,
    dist_hot,
    sizes,
    segs,
    stats,
    parts,
    flows,
    inbox,
    turned,
    carry,
    ahead,
    dest_send,
    dest_recv,
    orig_send,
    orig_recv,
    sum_send,
    sum_recv,
    back_send,
    back_recv,
    turn_send,
    skim_sem,
    load_sem,
):
    skim_count, rows, zones = skims.shape
    seg_count = theta.shape[1]
    mode_count = availability.shape[0]
    dist_count = district_const.shape[0]
    groups = rows // GROUP
    me_dest = lax.axis_index("dest")
    me_orig = lax.axis_index("orig")
    dest = [
        Exchange("dest", n_dest, dest_send.at[i], dest_recv.at[i], buf)
        for i, buf in enumerate((sizes, stats.at[0], stats.at[1]))
    ]
    orig = [
        Exchange("orig", n_orig, orig_send.at[i], orig_recv.at[i], buf)
        for i, buf in enumerate((segs, parts.at[0], parts.at[1]))
    ]

    barrier = pltpu.get_barrier_semaphore()
    for axis, me, count in (("dest", me_dest, n_dest), ("orig", me_orig, n_orig)):
        for k in range(1, count):
            pl.semaphore_signal(
                barrier,
                inc=1,
                device_id={axis: lax.rem(me + k, count)},
                device_id_type=MESH,
            )
    small = [
        (segment_hbm, segment),
        (workers_hbm, workers),
        (beta_hbm, beta),
        (employment_hbm, employment),
        (zone_district_hbm, zone_district),
        (coef_hbm, coef),
        (asc_hbm, asc),
        (availability_hbm, availability),
        (theta_hbm, theta),
        (anchor_district_hbm, anchor_district),
        (district_const_hbm, district_const),
    ]
    loads = [pltpu.make_async_copy(a, b, load_sem.at[i]) for i, (a, b) in enumerate(small)]

    def skim_load(g):
        part = pl.ds(pl.multiple_of(g * GROUP, GROUP), GROUP)
        return pltpu.make_async_copy(skims_hbm.at[:, part], skims.at[:, part], skim_sem.at[g])

    for load in loads:
        load.start()
    for g in range(groups):
        skim_load(g).start()
    for load in loads:
        load.wait()

    seg_hot_t = hot(segment[...] == iota((seg_count, rows), 0))
    worker_hot = seg_hot_t * workers[...]
    eye = hot(iota((rows, rows), 0) == iota((rows, rows), 1))
    seg_col = jnp.sum(eye * segment[...].astype(F32), axis=1, keepdims=True).astype(jnp.int32)
    seg_hot = hot(seg_col == iota((rows, seg_count), 1))
    size_term = jnp.zeros((seg_count, zones), F32)
    for c in range(beta.shape[1]):
        size_term = size_term + beta[:, c : c + 1] * employment[c : c + 1, :].astype(F32)
    sizes[me_dest] = jnp.broadcast_to(jnp.sum(size_term, axis=1, keepdims=True), sizes.shape[1:])
    segs[me_orig] = jnp.broadcast_to(jnp.sum(worker_hot, axis=1, keepdims=True), segs.shape[1:])
    dist_hot[...] = hot(zone_district[...] == iota((dist_count, zones), 0), BF16)

    def by_segment(table):
        out = jnp.zeros((rows, table.shape[1]), F32)
        for s in range(seg_count):
            out = jnp.where(seg_hot[:, s : s + 1] > 0.5, table[s : s + 1, :], out)
        return out

    block = mode_count * GROUP
    width = skim_count * GROUP
    wide = width + 2 * GROUP
    pair = seg_count * mode_count
    column = iota((1, 1, wide), 2)
    pair_eye = hot(iota((pair, pair), 0) == iota((pair, pair), 1))
    widen = hot(iota((skim_count, wide), 1) // GROUP == iota((skim_count, wide), 0), BF16)
    table = dot(dot_nt(pair_eye.astype(BF16), coef[...]).astype(BF16), widen)
    rest = jnp.sum(pair_eye * asc[...], axis=1, keepdims=True)
    for i in range(3):
        part = rest.astype(BF16).astype(F32)
        table = jnp.where(column[0] == width + GROUP + i, part, table)
        rest = rest - part
    table = table.astype(BF16)
    usable = jnp.logical_or(availability[...] > 0, iota((mode_count, rows), 0) == 0)
    closed = jnp.where(usable, 0.0, -1e30)
    keep = jnp.logical_or(
        column % GROUP == iota((1, GROUP, 1), 1), column >= width + GROUP
    )
    for g in range(groups):
        mine = slice(g * GROUP, (g + 1) * GROUP)
        lane_of = seg_col[mine].reshape(1, GROUP, 1) * mode_count + iota((mode_count, 1, 1), 0)
        row_pair = hot(lane_of == iota((1, 1, pair), 2)).reshape(block, pair)
        main = dot(row_pair.astype(BF16), table).reshape(mode_count, GROUP, wide)
        shut = jnp.concatenate(
            [
                jnp.zeros((mode_count, width), F32),
                closed[:, mine],
                jnp.zeros((mode_count, GROUP), F32),
            ],
            axis=1,
        )
        main = jnp.where(keep, main + shut.reshape(mode_count, 1, wide), 0.0)
        weights[g * block : (g + 1) * block, :] = main.reshape(block, wide).astype(BF16)
    ones = jnp.ones((2 * GROUP, TILE), BF16)

    theta_rows[...] = jnp.broadcast_to(
        jnp.sum(seg_hot * theta[...], axis=1, keepdims=True), theta_rows.shape
    )
    anchor_hot_t = hot(anchor_district[...] == iota((dist_count, rows), 0), BF16)
    anchor_hot = dot_nt(eye.astype(BF16), anchor_hot_t)
    anchor_const = dot(anchor_hot, district_const[...], HIGH)
    top, low = halves(anchor_const)
    rest = (anchor_const - top.astype(F32) - low.astype(F32)).astype(BF16)
    pair_const = dot(jnp.concatenate([top, low, rest], axis=0), dist_hot[...])
    pair_const = pair_const[:rows] + (pair_const[rows : 2 * rows] + pair_const[2 * rows :])
    base[...] = by_segment(jnp.log(size_term)) + pair_const

    def group_step(g, carry):
        first = pl.multiple_of(g * GROUP, GROUP)
        skim_load(g).wait()
        mine = pl.ds(pl.multiple_of(g * block, block), block)
        theta_col = theta_rows[pl.ds(first, GROUP), 0:1]
        for t in range(zones // TILE):
            cols = slice(t * TILE, (t + 1) * TILE)
            near = skims[:, pl.ds(first, GROUP), cols].reshape(width, TILE)
            near = jnp.concatenate([near, ones], axis=0)
            utility = dot(weights[mine, :], near).reshape(mode_count, GROUP, TILE)
            peak = jnp.max(utility, axis=0)
            grown = jnp.exp(utility - peak[None])
            total = jnp.sum(grown, axis=0)
            mode_exp[g, :, :, cols] = grown
            inv_total[pl.ds(first, GROUP), cols] = 1.0 / total
            base[pl.ds(first, GROUP), cols] += theta_col * (peak + jnp.log(total))
        return carry

    lax.fori_loop(0, groups, group_step, 0, unroll=True)

    pl.semaphore_wait(barrier, n_dest + n_orig - 2)

    def as_row(col):
        return jnp.sum(eye * col, axis=0, keepdims=True)

    def local_stats(value):
        peak = jnp.max(value, axis=1, keepdims=True)
        grown = jnp.exp(value - peak)
        total = jnp.sum(grown, axis=1, keepdims=True)
        stats[0, me_dest, 0:1, 0:rows] = as_row(peak)
        stats[0, me_dest, 1:2, 0:rows] = as_row(total)
        dest[1].share()
        dest[0].share()
        orig[0].share()
        return grown, peak

    def start_modelled(i, pieces, scale):
        left, left_low = halves(worker_hot * scale)
        both = dot(jnp.concatenate([left, left_low], axis=0), pieces[0])
        parts[i, me_orig] = both[:seg_count] + (dot(left, pieces[1]) + both[seg_count:])
        orig[1 + i].share()

    def end_modelled(i):
        orig[1 + i].landed()
        out = parts[i, 0]
        for j in range(1, n_orig):
            out = out + parts[i, j]
        return out

    grown, local_peak = local_stats(base[...])
    pieces = halves(grown)
    dest[0].landed()
    orig[0].landed()
    size_total, seg_total = sizes[0], segs[0]
    for j in range(1, n_dest):
        size_total = size_total + sizes[j]
    for j in range(1, n_orig):
        seg_total = seg_total + segs[j]
    target = size_term * (seg_total / size_total)[:, 0:1] + 1.0
    dest[1].landed()
    peaks = [stats[0, j, 0:1, 0:rows] for j in range(n_dest)]
    peak = functools.reduce(jnp.maximum, peaks)
    total = jnp.zeros_like(peak)
    for j in range(n_dest):
        total = total + stats[0, j, 1:2, 0:rows] * jnp.exp(peaks[j] - peak)
    start_modelled(0, pieces, jnp.exp(stats[0, me_dest, 0:1, 0:rows] - peak) / total)
    joint_peak = jnp.sum(eye * peak, axis=1, keepdims=True)
    grown = grown * jnp.exp(local_peak - joint_peak)
    base[...] = grown * inv_total[...]
    lanes = 2 * dist_count
    half = mode_count // 2
    width_out = dist_count * mode_count
    source = iota((2 * lanes, 1), 0)
    place = source % dist_count * mode_count + source // lanes
    place = place + source % lanes // dist_count * half
    starts = [(t, m) for t in range(0, width_out, TILE) for m in range(0, half, 2)]
    for i, (t, m) in enumerate(starts):
        spread[i] = hot(iota((2 * lanes, TILE), 1) == place + (m - t), BF16)
    ratio = target / (end_modelled(0) + 1.0)
    ratio_rows = by_segment(ratio)
    grown = grown * ratio_rows
    base[...] = base[...] * ratio_rows
    stats[1, me_dest, 0:1, 0:rows] = as_row(jnp.sum(grown, axis=1, keepdims=True))
    dest[2].share()

    half = mode_count // 2
    span = half // PIECES
    chunks = groups * PIECES
    size = span * GROUP
    middle = n_dest // 2
    odd = lax.rem(me_orig, 2) == 1
    inward = jnp.where(me_dest < middle, 1, -1)
    inner = jnp.logical_or(me_dest == middle - 1, me_dest == middle)
    outer = jnp.logical_and(me_dest != 0, me_dest != n_dest - 1)
    lane = jnp.where(inner, 1, 0)
    toward = me_dest + inward
    away = jnp.where(outer, me_dest - inward, toward)

    def rows_of(ref, c):
        return ref.at[pl.ds(pl.multiple_of(c * size, size), size)]

    def copy_in(c, slot, place, sem, device, source=flows):
        return pltpu.make_async_remote_copy(
            src_ref=rows_of(source, c),
            dst_ref=rows_of(inbox.at[slot], place),
            send_sem=sum_send.at[0],
            recv_sem=sum_recv.at[sem],
            device_id=device,
            device_id_type=MESH,
        )

    def sum_copy(c, slot, source=flows):
        return copy_in(c, n_dest + slot, c, slot * chunks + c, {"dest": toward}, source)

    def give_copy(c, source):
        sem = source * (chunks // 2) + c // 2
        return copy_in(c, source, c // 2, sem, {"dest": middle - 1 + c % 2})

    def first_copy(c):
        return copy_in(
            c,
            jnp.where(odd, n_dest + lane, me_dest),
            jnp.where(odd, c, c // 2),
            jnp.where(odd, lane * chunks + c, me_dest * (chunks // 2) + c // 2),
            {"dest": jnp.where(odd, toward, middle - 1 + c % 2)},
        )

    def back_copy(c):
        return pltpu.make_async_remote_copy(
            src_ref=rows_of(flow_out, c),
            dst_ref=rows_of(flow_out, c),
            send_sem=back_send.at[0],
            recv_sem=back_recv.at[0],
            device_id={"dest": away},
            device_id_type=MESH,
        )

    def other(i):
        return i + jnp.where(i >= me_dest, 1, 0)

    def turn_copy(k, i):
        c = 2 * k + me_dest - (middle - 1)
        return pltpu.make_async_remote_copy(
            src_ref=rows_of(flow_out, c),
            dst_ref=rows_of(flow_out, c),
            send_sem=turn_send.at[0],
            recv_sem=back_recv.at[0],
            device_id={"dest": other(i)},
            device_id_type=MESH,
        )

    def own_chunk(c):
        g, p = c // PIECES, c % PIECES
        factor = base[g * GROUP : (g + 1) * GROUP, :][None]
        mixed = jnp.concatenate(
            [
                mode_exp[g, k + p * span : k + (p + 1) * span] * factor
                for k in (0, half)
            ],
            axis=0,
        )
        top, low = halves(mixed.reshape(2 * size, zones))
        out = dot_nt(top, dist_hot[...]) + dot_nt(low, dist_hot[...])
        flows[c * size : (c + 1) * size, :] = jnp.concatenate([out[:size], out[size:]], axis=1)

    def joint_total():
        dest[2].landed()
        total = stats[1, 0, 0:1, 0:rows]
        for j in range(1, n_dest):
            total = total + stats[1, j, 0:1, 0:rows]
        start_modelled(1, halves(grown), 1.0 / total)
        access_out[...] = peak + jnp.log(total)
        scale = jnp.sum(eye * (workers[...] / total), axis=1, keepdims=True)
        scale_rows[...] = jnp.broadcast_to(scale, scale_rows.shape)

    def at(c):
        return slice(c * size, (c + 1) * size)

    def gather(c):
        sum_copy(c, 0).wait_recv()
        carry[at(c), :] = flows[at(c), :] + inbox[n_dest, at(c), :]
        sum_copy(c, lane, carry).start()

    def turn(c):
        sum_copy(c, 1).wait_recv()
        flow_out[at(c), :] = carry[at(c), :] + inbox[n_dest + 1, at(c), :]
        back_copy(c).start()

    def ahead_copy(c):
        return pltpu.make_async_remote_copy(
            src_ref=rows_of(ahead, c),
            dst_ref=rows_of(inbox.at[n_dest], c),
            send_sem=back_send.at[0],
            recv_sem=back_recv.at[0],
            device_id={"dest": 0},
            device_id_type=MESH,
        )

    def send_ahead(c):
        sum_copy(c, 1).wait_recv()
        ahead[at(c), :] = flows[at(c), :] + inbox[n_dest + 1, at(c), :]
        ahead_copy(c).start()

    def place_of(k):
        c = 2 * k + me_dest - (middle - 1)
        return pl.ds(pl.multiple_of(c * size, size), size)

    def early_copy(k):
        c = 2 * k + me_dest - (middle - 1)
        return pltpu.make_async_remote_copy(
            src_ref=rows_of(turned, k),
            dst_ref=rows_of(inbox.at[0], c),
            send_sem=turn_send.at[0],
            recv_sem=back_recv.at[0],
            device_id={"dest": 0},
            device_id_type=MESH,
        )

    def serve(k):
        for i in range(1, n_dest - 1):
            give_copy(2 * k, other(i)).wait_recv()
        both = flows[place_of(k), :]
        for i in range(1, n_dest - 1):
            both = both + inbox[other(i), at(k), :]
        turned[at(k), :] = both
        early_copy(k).start()

    def serve_rest(k):
        give_copy(2 * k, 0).wait_recv()
        flow_out[place_of(k), :] = turned[at(k), :] + inbox[0, at(k), :]
        for i in range(1, n_dest - 1):
            turn_copy(k, i).start()

    line_mid = jnp.logical_and(odd, outer)
    serves = jnp.logical_and(jnp.logical_not(odd), inner)
    short = jnp.int32(middle) == 2
    adds = jnp.logical_and(me_dest == 0, jnp.logical_or(jnp.logical_not(odd), short))
    plain = jnp.logical_not(jnp.logical_or(line_mid, serves))

    def not_mine(c):
        return me_dest != middle - 1 + c % 2

    @pl.when(line_mid)
    def _():
        for c in range(chunks):
            own_chunk(c)

    @pl.when(serves)
    def _():
        for c in range(chunks):
            own_chunk(c)
            pl.when(not_mine(c))(lambda c=c: first_copy(c).start())

        for k in range(chunks // 2):
            if k == WAIT:
                joint_total()
            serve(k)
        for k in range(chunks // 2):
            serve_rest(k)

    @pl.when(plain)
    def _():
        for c in range(chunks):
            own_chunk(c)
            first_copy(c).start()

    line_inner = jnp.logical_and(odd, inner)

    leads = jnp.logical_and(line_inner, jnp.logical_and(short, me_dest == 1))

    @pl.when(leads)
    def _():
        for c in range(chunks + LEAD):
            if c == WAIT:
                joint_total()
            if c < chunks:
                gather(c)
            if c >= LEAD:
                send_ahead(c - LEAD)
        flow_out[...] = carry[...] + inbox[n_dest + 1]

    @pl.when(jnp.logical_and(line_inner, jnp.logical_not(leads)))
    def _():
        for c in range(chunks + LAG):
            if c == WAIT:
                joint_total()
            if c < chunks:
                gather(c)
            if c >= LAG:
                turn(c - LAG)

    @pl.when(jnp.logical_not(inner))
    def _():
        joint_total()

        @pl.when(line_mid)
        def _():
            for c in range(chunks):
                gather(c)

    modelled = end_modelled(1)
    modelled_out[...] = modelled
    shadow_out[...] = jnp.log(ratio) + jnp.log(target / (modelled + 1.0))

    def amount(ref, send, recv):
        return pltpu.make_async_remote_copy(
            src_ref=ref,
            dst_ref=ref,
            send_sem=send.at[0],
            recv_sem=recv.at[0],
            device_id={"dest": away},
            device_id_type=MESH,
        )

    @pl.when(jnp.logical_not(jnp.logical_or(line_inner, serves)))
    def _():
        amount(flow_out, back_send, back_recv).wait_recv()

        @pl.when(line_mid)
        def _():
            amount(flow_out, back_send, back_recv).start()

        @pl.when(adds)
        def _():
            flow_out[...] = flows[...] + inbox[jnp.where(odd, n_dest, 0)]

    @pl.when(serves)
    def _():
        amount(turned, sum_send, back_recv).wait_recv()
        amount(turned, sum_send, back_recv).wait_send()
        sent = inbox.at[pl.ds(0, n_dest - 1), pl.ds(0, turned.shape[0])]
        amount(sent, turn_send, back_recv).wait_send()

    @pl.when(jnp.logical_not(serves))
    def _():
        amount(flows, sum_send, back_recv).wait_send()

    @pl.when(line_mid)
    def _():
        amount(flow_out, back_send, back_recv).wait_send()

    for one in dest + orig:
        one.sent()


def finish(
    mode_count, groups, flow, access, modelled, shadow, scale, spread, flow_out, access_out,
    modelled_out, shadow_out, table, sem, table_sem,
):
    copies = [
        pltpu.make_async_copy(a, b, sem.at[i])
        for i, (a, b) in enumerate(
            ((access, access_out), (modelled, modelled_out), (shadow, shadow_out))
        )
    ]
    for copy in copies:
        copy.start()
    lanes = flow.shape[1]
    half = mode_count // 2
    rows = groups * GROUP
    width = table.shape[1]
    starts = [(t, m) for t in range(0, width, TILE) for m in range(0, half, 2)]
    pieces = flow[...].reshape(groups, half, GROUP, lanes)
    pieces = pieces * scale[...].reshape(groups, 1, GROUP, lanes)
    pairs = []
    for m in range(0, half, 2):
        pair = [pieces[:, m + i].reshape(rows, lanes) for i in range(2)]
        pairs.append(jnp.concatenate(halves(jnp.concatenate(pair, axis=1)), axis=0))
    for t in range(0, width, TILE):
        total = jnp.zeros((2 * rows, TILE), F32)
        for i, (start, m) in enumerate(starts):
            if start == t:
                total = total + dot(pairs[m // 2], spread[i])
        cols = slice(t, t + TILE)
        table[:, cols] = total[:rows] + total[rows:]
        copy = pltpu.make_async_copy(
            table.at[:, cols], flow_out.at[:, cols], table_sem.at[t // TILE]
        )
        copy.start()
        copies.append(copy)
    for copy in copies:
        copy.wait()


def per_device(
    n_dest,
    n_orig,
    skims,
    coef,
    asc,
    theta,
    beta,
    employment,
    zone_district,
    anchor_district,
    district_const,
    segment,
    availability,
    workers,
):
    skim_count, rows, zones = skims.shape
    seg_count = theta.shape[0]
    mode_count = availability.shape[1]
    dist_count = district_const.shape[0]
    groups = rows // GROUP
    inputs = (
        skims,
        coef.T,
        asc.reshape(1, -1),
        theta.reshape(1, -1),
        beta,
        employment,
        zone_district.reshape(1, -1),
        anchor_district.reshape(1, -1),
        district_const,
        segment.reshape(1, -1),
        availability.T,
        workers.reshape(1, -1),
    )
    flow_rows = rows * mode_count // 2
    lanes = max(128, rows)
    chunks = groups * PIECES
    width = dist_count * mode_count
    vmem = pl.BlockSpec(memory_space=pltpu.VMEM)
    sem = pltpu.SemaphoreType.DMA
    access, flow, modelled, shadow, scale, spread = pl.pallas_call(
        functools.partial(kernel, n_dest, n_orig),
        out_shape=(
            pltpu.VMEM((1, rows), F32),
            pltpu.VMEM((flow_rows, 2 * dist_count), F32),
            pltpu.VMEM((seg_count, zones), F32),
            pltpu.VMEM((seg_count, zones), F32),
            pltpu.VMEM((rows, 2 * dist_count), F32),
            pltpu.VMEM((width // TILE * (mode_count // 4), 4 * dist_count, TILE), BF16),
        ),
        in_specs=[pl.BlockSpec(memory_space=pl.ANY)] * 12,
        out_specs=(vmem,) * 6,
        scratch_shapes=[pltpu.VMEM(x.shape, x.dtype) for x in inputs]
        + [
            pltpu.VMEM((groups, mode_count, GROUP, zones), F32),
            pltpu.VMEM((rows, zones), F32),
            pltpu.VMEM((rows * mode_count, (skims.shape[0] + 2) * GROUP), BF16),
            pltpu.VMEM((rows, 128), F32),
            pltpu.VMEM((rows, zones), F32),
            pltpu.VMEM((dist_count, zones), BF16),
            pltpu.VMEM((n_dest, seg_count, 128), F32),
            pltpu.VMEM((n_orig, seg_count, 128), F32),
            pltpu.VMEM((2, n_dest, 8, lanes), F32),
            pltpu.VMEM((2, n_orig, seg_count, zones), F32),
            pltpu.VMEM((flow_rows, 2 * dist_count), F32),
            pltpu.VMEM((n_dest + 2, flow_rows, 2 * dist_count), F32),
            pltpu.VMEM((flow_rows // 2, 2 * dist_count), F32),
            pltpu.VMEM((flow_rows, 2 * dist_count), F32),
            pltpu.VMEM((flow_rows, 2 * dist_count), F32),
            sem((3,)),
            sem((3,)),
            sem((3,)),
            sem((3,)),
            sem((1,)),
            sem((max(n_dest * (chunks // 2), 2 * chunks),)),
            sem((1,)),
            sem((1,)),
            sem((1,)),
            sem((groups,)),
            sem((len(inputs) - 1,)),
        ],
        compiler_params=pltpu.CompilerParams(
            collective_id=0, has_side_effects=True, vmem_limit_bytes=33554432
        ),
    )(*(pltpu.with_memory_space_constraint(x, pltpu.HBM) for x in inputs))
    anywhere = pl.BlockSpec(memory_space=pl.ANY)
    results = [
        pltpu.with_memory_space_constraint(x, pltpu.VMEM)
        for x in (flow, access, modelled, shadow, scale, spread)
    ]
    flow, access, modelled, shadow = pl.pallas_call(
        functools.partial(finish, mode_count, groups),
        out_shape=(jax.ShapeDtypeStruct((rows, dist_count * mode_count), F32),)
        + tuple(jax.ShapeDtypeStruct(x.shape, x.dtype) for x in results[1:4]),
        in_specs=[vmem] * 6,
        out_specs=(anywhere,) * 4,
        scratch_shapes=[
            pltpu.VMEM((rows, width), F32),
            sem((3,)),
            sem((width // TILE,)),
        ],
        compiler_params=pltpu.CompilerParams(vmem_limit_bytes=16777216),
    )(*results)
    return access.reshape(rows), flow, modelled, shadow


def solution(mesh):
    return jax.shard_map(
        functools.partial(per_device, mesh.shape["dest"], mesh.shape["orig"]),
        mesh=mesh,
        in_specs=(
            P(None, ("scen", "orig"), "dest"),
            P(),
            P(),
            P(),
            P(),
            P(None, ("scen", "dest")),
            P("dest"),
            P(("scen", "orig")),
            P(),
            P(("scen", "orig")),
            P(("scen", "orig"), None),
            P(("scen", "orig")),
        ),
        out_specs=(
            P(("scen", "orig")),
            P(("scen", "orig"), None),
            P(None, ("scen", "dest")),
            P(None, ("scen", "dest")),
        ),
        check_vma=False,
    )
```
